128 devices in a mesh: copy: 2 (over x_hi), ctx: 32 (over y, z, x_lo), tp: 2 (over core).
Axes of the slice: x: 4 (x_hi: 2, x_lo: 2; x = x_hi * 2 + x_lo), y: 4, z: 4, core: 2. Of those that a mesh axis runs over, the one named last changes fastest.
Arguments:
- clean_tokens: bfloat16 [8192, 4096], P('ctx', 'copy'), may hold values from -36 to 36
- norm_gain: bfloat16 [4096], replicated, may hold values from 0.5 to 1.5
- mask_embed: bfloat16 [4096], replicated, may hold values from -6 to 6
- time_shift: float32 [4096], replicated, may hold values from -0.5 to 0.5
- w_query: bfloat16 [4096, 2048], P(None, 'tp'), may hold values from -0.09375 to 0.09375
- w_key: bfloat16 [4096, 512], P(None, 'tp'), may hold values from -0.09375 to 0.09375
- w_value: bfloat16 [4096, 512], P(None, 'tp'), may hold values from -0.09375 to 0.09375
- w_out: bfloat16 [2048, 4096], P('tp'), may hold values from -0.125 to 0.125
- q_gain: float32 [128], replicated, may hold values from 2 to 3
- k_gain: float32 [128], replicated, may hold values from 0.5 to 1.5
- masked: int32 [2, 8192], P('copy', 'ctx'), may hold values 0 or 1
- block_live: int32 [2, 128], P('copy', 'ctx'), may hold values 0 or 1
- timesteps: int32 [2], P('copy'), may hold values from 1 to 1000
Outputs:
- clean_out: bfloat16 [8192, 4096], P('ctx', 'tp')
- noised_out: bfloat16 [2, 8192, 4096], P('copy', 'ctx', 'tp')
The draws below stay inside these ranges and needn't reach their ends.
All inputs are finite; a program needn't handle non-finite values. No bound on the sum of `masked` or of `block_live` on one device may be relied on, other than what follows from the above.
Results may differ from the reference program's by a relative error of at most 0.012.
The reference program's roundings to bfloat16 on the way count: a program that leaves them out, or rounds other values in their place, can miss the bound.
Values may be sent and summed in bfloat16 or wider, within the bound.
A program may use at most 320 MiB of HBM per device.

```python
import math
import jax
import jax.numpy as jnp
from jax import lax

D = 4096
H = 16
KVH = 4
HD = 128
BLK = 64
TSTEPS = 1000
SEQ = 8192
NBLK = 128
COPIES = 2


def draw_clean_tokens(key, part):
    key_base = jax.random.fold_in(key, 101)
    key_lines = jax.random.fold_in(key, 102)
    key_features = jax.random.fold_in(key, 103)
    line_scale = jnp.exp(jax.random.uniform(key_lines, (SEQ, 1), minval=math.log(0.3), maxval=math.log(3.0)))
    feature_scale = jnp.exp(jax.random.uniform(key_features, (1, D), minval=math.log(0.3), maxval=math.log(3.0)))
    base = jnp.clip(jax.random.normal(key_base, (SEQ, D)), -4.0, 4.0)
    return (base * line_scale * feature_scale).astype(jnp.bfloat16)


def set_ends(values, rng, smallest, top_value):
    index_at = [jax.random.randint(jax.random.fold_in(rng, axis), (), 0, length) for axis, length in enumerate(values.shape)]
    longest = values.shape.index(max(values.shape))
    next_to = index_at[:longest] + [(index_at[longest] + 1) % values.shape[longest]] + index_at[longest + 1:]
    return values.at[tuple(index_at)].set(smallest).at[tuple(next_to)].set(top_value)


def steps_of(rng, dims, pieces, least, top_value):
    def one(dim, shards_of):
        steps = jax.random.uniform(jax.random.fold_in(jax.random.fold_in(rng, 6), dim), (shards_of,), jnp.float32, least / len(pieces), top_value / len(pieces))
        return jnp.repeat(jnp.exp(steps), dims[dim] // shards_of).reshape((-1,) + (1,) * (len(dims) - dim - 1))

    level = one(*pieces[0])
    for cut in pieces[1:]:
        level = level * one(*cut)
    return level


def scatter_about(own_key, shape, deviation, bound, split=(), kind=jnp.bfloat16):
    result = jax.random.normal(own_key, shape, jnp.float32) * deviation
    if len(split) > 0:
        result = steps_of(own_key, shape, split, -0.22, 0.18) * result
    return jnp.clip(result, min=-bound, max=bound).astype(kind)


def setup_inputs(seed: int = 0) -> dict:
    splits = jax.random.split(jax.random.key(seed), 14)
    clean_tokens = draw_clean_tokens(jax.random.fold_in(splits[13], 71), 0)
    norm_gain = jnp.clip(1.0 + 0.1 * jax.random.normal(splits[1], (D,), jnp.float32), 0.5, 1.5).astype(jnp.bfloat16)
    mask_embed = scatter_about(splits[2], (D,), 1.0, 6.0)
    time_shift = jnp.clip(jax.random.uniform(splits[3], (D,), jnp.float32, -0.5, 0.5), -0.5, 0.5)
    w_query = scatter_about(splits[4], (D, H * HD), D ** -0.5, 0.09375, ((1, 2),))
    w_key = scatter_about(splits[5], (D, KVH * HD), D ** -0.5, 0.09375, ((1, 2),))
    w_value = scatter_about(splits[6], (D, KVH * HD), D ** -0.5, 0.09375, ((1, 2),))
    w_out = scatter_about(splits[7], (H * HD, D), (H * HD) ** -0.5, 0.125, ((0, 2),))
    q_gain = jnp.clip(jax.random.uniform(splits[8], (HD,), jnp.float32, 2.0, 3.0), 2.0, 3.0)
    k_gain = jnp.clip(1.0 + 0.1 * jax.random.normal(splits[9], (HD,), jnp.float32), 0.5, 1.5)
    masked = set_ends((jax.random.randint(splits[10], (COPIES, SEQ), 0, 2) < 1).astype(jnp.int32), jax.random.fold_in(splits[10], 1), 0, 1)
    block_live = set_ends((jax.random.randint(splits[11], (COPIES, NBLK), 0, 4) < 3).astype(jnp.int32), jax.random.fold_in(splits[11], 1), 0, 1)
    timesteps = jax.random.randint(splits[12], (COPIES,), 1, 1001).astype(jnp.int32)
    return {"clean_tokens": clean_tokens, "norm_gain": norm_gain, "mask_embed": mask_embed, "time_shift": time_shift, "w_query": w_query, "w_key": w_key, "w_value": w_value, "w_out": w_out, "q_gain": q_gain, "k_gain": k_gain, "masked": masked, "block_live": block_live, "timesteps": timesteps}


EPS = 1e-06

def inverse_rms(values):
    return lax.rsqrt(lax.optimization_barrier(jnp.mean(values * values, axis=-1, keepdims=True)) + EPS)

def reference(clean_tokens, norm_gain, mask_embed, time_shift, w_query, w_key, w_value, w_out, q_gain, k_gain, masked, block_live, timesteps):
    streams_count = 1 + COPIES
    clean_wide = clean_tokens.astype(jnp.float32)
    gain_wide = norm_gain.astype(jnp.float32)
    normed_clean = (clean_wide * inverse_rms(clean_wide) * gain_wide).astype(jnp.bfloat16)
    noisy_tokens = jnp.where(masked[:, :, None] == 1, mask_embed[None, None, :], clean_tokens[None, :, :])
    noisy_wide = noisy_tokens.astype(jnp.float32)
    condition = 1.0 + timesteps.astype(jnp.float32)[:, None, None] / TSTEPS * time_shift[None, None, :]
    normed_noisy = (noisy_wide * inverse_rms(noisy_wide) * gain_wide * condition).astype(jnp.bfloat16)
    all_rows = jnp.concatenate([normed_clean[None], normed_noisy], axis=0).reshape(-1, D)
    query_wide = jnp.dot(all_rows, w_query, preferred_element_type=jnp.float32).reshape(streams_count, SEQ, H, HD)
    queries = (query_wide * inverse_rms(query_wide) * q_gain).astype(jnp.bfloat16)
    key_wide = jnp.dot(all_rows, w_key, preferred_element_type=jnp.float32).reshape(streams_count, SEQ, KVH, HD)
    key_heads = (key_wide * inverse_rms(key_wide) * k_gain).astype(jnp.bfloat16)
    value_heads = jnp.dot(all_rows, w_value, preferred_element_type=jnp.float32).astype(jnp.bfloat16).reshape(streams_count, SEQ, KVH, HD)
    blocks = jnp.arange(SEQ, dtype=jnp.int32) // BLK
    heads_per_kv = H // KVH
    reciprocal_root = 1.0 / math.sqrt(HD)

    def one_head(pair_index):
        stream_index = pair_index // H
        head_index = pair_index % H
        kv_head = head_index // heads_per_kv
        query_rows = queries[stream_index, :, head_index, :].astype(jnp.float32)
        clean_key = key_heads[0, :, kv_head, :].astype(jnp.float32)
        clean_value = value_heads[0, :, kv_head, :].astype(jnp.float32)
        scores = jnp.dot(query_rows, clean_key.T) * reciprocal_root
        offset = jnp.minimum(stream_index, 1)
        allowed = blocks[None, :] + offset <= blocks[:, None]
        weights = jnp.where(allowed, jnp.exp(scores), 0.0)
        numerator = jnp.dot(weights.astype(jnp.bfloat16).astype(jnp.float32), clean_value)
        denominator = lax.optimization_barrier(jnp.sum(weights, axis=1))
        self_block_key = key_heads[stream_index, :, kv_head, :].astype(jnp.float32).reshape(NBLK, BLK, HD)
        self_block_value = value_heads[stream_index, :, kv_head, :].astype(jnp.float32).reshape(NBLK, BLK, HD)
        self_block_query = query_rows.reshape(NBLK, BLK, HD)
        self_block_scores = jnp.einsum('xau,xvu->xav', self_block_query, self_block_key) * reciprocal_root
        own_flag = offset.astype(jnp.float32)
        self_block_weights = jnp.exp(self_block_scores) * own_flag
        self_numerator = jnp.einsum('osf,ofg->osg', self_block_weights.astype(jnp.bfloat16).astype(jnp.float32), self_block_value)
        numerator = numerator + self_numerator.reshape(SEQ, HD)
        denominator = denominator + lax.optimization_barrier(jnp.sum(self_block_weights, axis=2)).reshape(SEQ)
        return (numerator / denominator[:, None]).astype(jnp.bfloat16)
    attended = lax.map(one_head, jnp.arange(streams_count * H, dtype=jnp.int32))
    attended = attended.reshape(streams_count, H, SEQ, HD).transpose(0, 2, 1, 3).reshape(streams_count * SEQ, H * HD)
    mixed = jnp.dot(attended, w_out, preferred_element_type=jnp.float32)
    clean_out = mixed[:SEQ].astype(jnp.bfloat16)
    live_rows = jnp.repeat(block_live, BLK, axis=1).astype(jnp.float32)
    noised_out = (mixed[SEQ:].reshape(COPIES, SEQ, D) * live_rows[:, :, None]).astype(jnp.bfloat16)
    return (clean_out, noised_out)
```

```python
import functools
import math

import jax
import jax.numpy as jnp
from jax import lax
from jax.experimental import pallas as pl
from jax.experimental.pallas import tpu as pltpu
from jax.sharding import PartitionSpec as P

HD = 128
BLK = 64
TSTEPS = 1000
EPS = 1e-06
GROUP = 4


def inverse_rms(values):
    return lax.rsqrt(jnp.mean(values * values, axis=-1, keepdims=True) + EPS)


def attend_kernel(rows, heads, streams, raw_ref, gain_ref, own_ref, kv_ref, out_ref, q_ref, acc_ref):
    me = lax.axis_index("ctx")
    scale = math.log2(math.e) / math.sqrt(HD)
    gain = gain_ref[...]
    query_block = lax.broadcasted_iota(jnp.int32, (rows, rows), 0) // BLK
    key_block = lax.broadcasted_iota(jnp.int32, (rows, rows), 1) // BLK

    def split(kv):
        ones = jnp.ones((kv.shape[0], HD), jnp.bfloat16)
        return kv[:, :HD], jnp.concatenate([kv[:, HD:], ones], axis=1)

    def exponentials(queries, keys):
        scores = lax.dot_general(
            queries, keys, (((1,), (1,)), ((), ())), preferred_element_type=jnp.float32
        )
        return jnp.exp2(scores * scale)

    keys, values = split(own_ref[0])
    for stream in range(streams):
        if stream:
            self_keys, self_values = split(own_ref[stream])
        for head in range(heads):
            raw = raw_ref[stream * rows : (stream + 1) * rows, head * HD : (head + 1) * HD]
            queries = (raw * inverse_rms(raw) * gain).astype(jnp.bfloat16)
            at = pl.ds((stream * heads + head) * rows, rows)
            q_ref[at] = queries
            allowed = key_block < query_block if stream else key_block <= query_block
            weights = jnp.where(allowed, exponentials(queries, keys), 0.0).astype(jnp.bfloat16)
            total = jnp.dot(weights, values, preferred_element_type=jnp.float32)
            if stream:
                weights = jnp.where(
                    key_block == query_block, exponentials(queries, self_keys), 0.0
                ).astype(jnp.bfloat16)
                total += jnp.dot(weights, self_values, preferred_element_type=jnp.float32)
            acc_ref[at] = total

    def accumulate(start, count):
        group_keys, group_values = split(kv_ref[pl.ds(start, count)].reshape(count * rows, 2 * HD))
        for tile in range(streams * heads):
            at = pl.ds(tile * rows, rows)
            weights = exponentials(q_ref[at], group_keys).astype(jnp.bfloat16)
            acc_ref[at] += jnp.dot(weights, group_values, preferred_element_type=jnp.float32)

    def whole(step, carry):
        accumulate(step * GROUP, GROUP)
        return carry

    def single(step, carry):
        accumulate(step, 1)
        return carry

    lax.fori_loop(0, me // GROUP, whole, 0)
    lax.fori_loop(me // GROUP * GROUP, me, single, 0)
    for stream in range(streams):
        for head in range(heads):
            at = pl.ds((stream * heads + head) * rows, rows)
            out_ref[stream * rows : (stream + 1) * rows, head * HD : (head + 1) * HD] = (
                acc_ref[at, :HD] / acc_ref[at, HD:]
            ).astype(jnp.bfloat16)


def attend(raw, q_gain, own, kv, streams, rows, heads):
    return pl.pallas_call(
        functools.partial(attend_kernel, rows, heads, streams),
        out_shape=jax.ShapeDtypeStruct((streams * rows, heads * HD), jnp.bfloat16),
        in_specs=[pl.BlockSpec(memory_space=pltpu.VMEM)] * 4,
        out_specs=pl.BlockSpec(memory_space=pltpu.VMEM),
        scratch_shapes=[
            pltpu.VMEM((streams * heads * rows, HD), jnp.bfloat16),
            pltpu.VMEM((streams * heads * rows, 2 * HD), jnp.float32),
        ],
        compiler_params=pltpu.CompilerParams(vmem_limit_bytes=48 * 2**20),
    )(raw, q_gain, own, kv)


SWAP = [(0, 1), (1, 0)]


def on_device(
    clean_tokens,
    norm_gain,
    mask_embed,
    time_shift,
    w_query,
    w_key,
    w_value,
    w_out,
    q_gain,
    k_gain,
    masked,
    block_live,
    timesteps,
):
    mine = lax.axis_index("copy")
    core = lax.axis_index("tp")
    first = mine == 0
    rows = clean_tokens.shape[0]
    streams = 3
    q_width = w_query.shape[1] // 2
    heads = q_width // HD

    def ordered(own, other, axis):
        return jnp.where(
            first,
            jnp.concatenate([own, other], axis=axis),
            jnp.concatenate([other, own], axis=axis),
        )

    notes = jnp.concatenate([masked, timesteps[:, None]], axis=1)
    other_notes = lax.ppermute(notes, "copy", SWAP)
    other_tokens = lax.ppermute(clean_tokens, "copy", SWAP)
    weights = jnp.concatenate(
        [
            lax.dynamic_slice_in_dim(w_query, mine * q_width, q_width, axis=1),
            lax.dynamic_slice_in_dim(w_key, mine * HD, HD, axis=1),
            lax.dynamic_slice_in_dim(w_value, mine * HD, HD, axis=1),
        ],
        axis=1,
    )
    features = ordered(clean_tokens, other_tokens, 1).astype(jnp.float32)
    both_notes = ordered(notes, other_notes, 0)
    gain = norm_gain.astype(jnp.float32)
    base = features * inverse_rms(features) * gain
    mask_wide = mask_embed.astype(jnp.float32)[None, :]
    mask_base = mask_wide * inverse_rms(mask_wide) * gain
    condition = (
        1.0 + both_notes[:, rows:].astype(jnp.float32)[:, :, None] / TSTEPS * time_shift[None, None, :]
    )
    noisy = jnp.where(both_notes[:, :rows, None] == 1, mask_base[None], base[None]) * condition
    all_rows = jnp.concatenate([base[None], noisy], axis=0).astype(jnp.bfloat16)
    wide = jnp.dot(
        all_rows.reshape(streams * rows, -1), weights, preferred_element_type=jnp.float32
    )
    raw = wide[:, :q_width]
    key_wide = wide[:, q_width : q_width + HD]
    keys = (key_wide * inverse_rms(key_wide) * k_gain).astype(jnp.bfloat16)
    values = wide[:, q_width + HD :].astype(jnp.bfloat16)
    own = jnp.concatenate([keys, values], axis=1).reshape(streams, rows, 2 * HD)
    kv = lax.all_gather(own[0], "ctx", axis=0)
    attended = attend(raw, q_gain[None, :], own, kv, streams, rows, heads)
    attended = attended.reshape(streams, rows, q_width)
    kept = jnp.concatenate(
        [attended[:1], lax.dynamic_slice_in_dim(attended, 1 + mine, 1, axis=0)], axis=0
    )
    given = jnp.concatenate(
        [attended[:1], lax.dynamic_slice_in_dim(attended, 2 - mine, 1, axis=0)], axis=0
    )
    taken = lax.ppermute(given, "copy", SWAP)
    head_rows = ordered(kept, taken, 2).reshape(2 * rows, 2 * q_width)
    half = w_out.shape[1] // 2
    away = lax.dynamic_slice_in_dim(w_out, (1 - core) * half, half, axis=1)
    here = lax.dynamic_slice_in_dim(w_out, core * half, half, axis=1)
    sent = jnp.dot(head_rows, away, preferred_element_type=jnp.float32).astype(jnp.bfloat16)
    received = lax.ppermute(sent, "tp", SWAP)
    mixed = jnp.dot(head_rows, here, preferred_element_type=jnp.float32) + received.astype(
        jnp.float32
    )
    clean_out = mixed[:rows].astype(jnp.bfloat16)
    live_rows = jnp.repeat(block_live, BLK, axis=1).astype(jnp.float32)
    noised_out = (mixed[None, rows:] * live_rows[:, :, None]).astype(jnp.bfloat16)
    return (clean_out, noised_out)


def solution(mesh):
    in_specs = (
        P("ctx", "copy"),
        P(),
        P(),
        P(),
        P(None, "tp"),
        P(None, "tp"),
        P(None, "tp"),
        P("tp", None),
        P(),
        P(),
        P("copy", "ctx"),
        P("copy", "ctx"),
        P("copy"),
    )
    out_specs = (P("ctx", "tp"), P("copy", "ctx", "tp"))
    return jax.shard_map(
        on_device, mesh=mesh, in_specs=in_specs, out_specs=out_specs, check_vma=False
    )
```

```python
import functools
import math

import jax
import jax.numpy as jnp
from jax import lax
from jax.experimental import pallas as pl
from jax.experimental.pallas import tpu as pltpu
from jax.sharding import PartitionSpec as P

HD = 128
BLK = 64
TSTEPS = 1000
EPS = 1e-06
GROUP = 4
MESH = pl.DeviceIdType.MESH


def inverse_rms(values):
    return lax.rsqrt(jnp.mean(values * values, axis=-1, keepdims=True) + EPS)


def attend_kernel(
    rows, heads, streams, spans, raw_ref, gain_ref, own_ref, out_ref, kv_ref, q_ref, acc_ref, send_sem, recv_sem
):
    me = lax.axis_index("ctx")

    barrier = pltpu.get_barrier_semaphore()

    def greet(step, carry):
        pl.semaphore_signal(
            barrier, inc=1, device_id={"ctx": lax.rem(me + step, spans)}, device_id_type=MESH
        )
        return carry

    lax.fori_loop(1, spans, greet, 0)
    pl.semaphore_wait(barrier, spans - 1)

    def push(target):
        return pltpu.make_async_remote_copy(
            src_ref=own_ref.at[0],
            dst_ref=kv_ref.at[me],
            send_sem=send_sem.at[target],
            recv_sem=recv_sem.at[me],
            device_id={"ctx": target},
            device_id_type=MESH,
        )

    def arrival(source):
        return pltpu.make_async_remote_copy(
            src_ref=own_ref.at[0],
            dst_ref=kv_ref.at[source],
            send_sem=send_sem.at[source],
            recv_sem=recv_sem.at[source],
            device_id={"ctx": source},
            device_id_type=MESH,
        )

    def start_push(target, carry):
        push(target).start()
        return carry

    def end_push(target, carry):
        push(target).wait_send()
        return carry

    lax.fori_loop(me + 1, spans, start_push, 0)
    scale = math.log2(math.e) / math.sqrt(HD)
    gain = gain_ref[...]
    query_block = lax.broadcasted_iota(jnp.int32, (rows, rows), 0) // BLK
    key_block = lax.broadcasted_iota(jnp.int32, (rows, rows), 1) // BLK

    def split(kv):
        ones = jnp.ones((kv.shape[0], HD), jnp.bfloat16)
        return kv[:, :HD], jnp.concatenate([kv[:, HD:], ones], axis=1)

    def exponentials(queries, keys):
        scores = lax.dot_general(
            queries, keys, (((1,), (1,)), ((), ())), preferred_element_type=jnp.float32
        )
        return jnp.exp2(scores * scale)

    keys, values = split(own_ref[0])
    for stream in range(streams):
        if stream:
            self_keys, self_values = split(own_ref[stream])
        for head in range(heads):
            raw = raw_ref[stream * rows : (stream + 1) * rows, head * HD : (head + 1) * HD]
            queries = (raw * inverse_rms(raw) * gain).astype(jnp.bfloat16)
            at = pl.ds((stream * heads + head) * rows, rows)
            q_ref[at] = queries
            allowed = key_block < query_block if stream else key_block <= query_block
            weights = jnp.where(allowed, exponentials(queries, keys), 0.0).astype(jnp.bfloat16)
            total = jnp.dot(weights, values, preferred_element_type=jnp.float32)
            if stream:
                weights = jnp.where(
                    key_block == query_block, exponentials(queries, self_keys), 0.0
                ).astype(jnp.bfloat16)
                total += jnp.dot(weights, self_values, preferred_element_type=jnp.float32)
            acc_ref[at] = total

    def accumulate(start, count):
        for offset in range(count):
            arrival(start + offset).wait_recv()
        group_keys, group_values = split(kv_ref[pl.ds(start, count)].reshape(count * rows, 2 * HD))
        for tile in range(streams * heads):
            at = pl.ds(tile * rows, rows)
            weights = exponentials(q_ref[at], group_keys).astype(jnp.bfloat16)
            acc_ref[at] += jnp.dot(weights, group_values, preferred_element_type=jnp.float32)

    def whole(step, carry):
        accumulate(me - (step + 1) * GROUP, GROUP)
        return carry

    def single(step, carry):
        accumulate(lax.rem(me, GROUP) - 1 - step, 1)
        return carry

    lax.fori_loop(0, me // GROUP, whole, 0)
    lax.fori_loop(0, lax.rem(me, GROUP), single, 0)
    for stream in range(streams):
        for head in range(heads):
            at = pl.ds((stream * heads + head) * rows, rows)
            out_ref[stream * rows : (stream + 1) * rows, head * HD : (head + 1) * HD] = (
                acc_ref[at, :HD] / acc_ref[at, HD:]
            ).astype(jnp.bfloat16)
    lax.fori_loop(me + 1, spans, end_push, 0)


def attend(raw, q_gain, own, streams, rows, heads, spans):
    return pl.pallas_call(
        functools.partial(attend_kernel, rows, heads, streams, spans),
        out_shape=jax.ShapeDtypeStruct((streams * rows, heads * HD), jnp.bfloat16),
        in_specs=[pl.BlockSpec(memory_space=pltpu.VMEM)] * 3,
        out_specs=pl.BlockSpec(memory_space=pltpu.VMEM),
        scratch_shapes=[
            pltpu.VMEM((spans, rows, 2 * HD), jnp.bfloat16),
            pltpu.VMEM((streams * heads * rows, HD), jnp.bfloat16),
            pltpu.VMEM((streams * heads * rows, 2 * HD), jnp.float32),
            pltpu.SemaphoreType.DMA((spans,)),
            pltpu.SemaphoreType.DMA((spans,)),
        ],
        compiler_params=pltpu.CompilerParams(
            vmem_limit_bytes=48 * 2**20, collective_id=0, has_side_effects=True
        ),
    )(raw, q_gain, own)


SWAP = [(0, 1), (1, 0)]


def on_device(
    clean_tokens,
    norm_gain,
    mask_embed,
    time_shift,
    w_query,
    w_key,
    w_value,
    w_out,
    q_gain,
    k_gain,
    masked,
    block_live,
    timesteps,
):
    mine = lax.axis_index("copy")
    core = lax.axis_index("tp")
    first = mine == 0
    rows = clean_tokens.shape[0]
    streams = 3
    q_width = w_query.shape[1] // 2
    heads = q_width // HD

    def ordered(own, other, axis):
        return jnp.where(
            first,
            jnp.concatenate([own, other], axis=axis),
            jnp.concatenate([other, own], axis=axis),
        )

    notes = jnp.concatenate([masked, timesteps[:, None]], axis=1)
    other_notes = lax.ppermute(notes, "copy", SWAP)
    other_tokens = lax.ppermute(clean_tokens, "copy", SWAP)
    weights = jnp.concatenate(
        [
            lax.dynamic_slice_in_dim(w_query, mine * q_width, q_width, axis=1),
            lax.dynamic_slice_in_dim(w_key, mine * HD, HD, axis=1),
            lax.dynamic_slice_in_dim(w_value, mine * HD, HD, axis=1),
        ],
        axis=1,
    )
    features = ordered(clean_tokens, other_tokens, 1).astype(jnp.float32)
    both_notes = ordered(notes, other_notes, 0)
    gain = norm_gain.astype(jnp.float32)
    base = features * inverse_rms(features) * gain
    mask_wide = mask_embed.astype(jnp.float32)[None, :]
    mask_base = mask_wide * inverse_rms(mask_wide) * gain
    condition = (
        1.0 + both_notes[:, rows:].astype(jnp.float32)[:, :, None] / TSTEPS * time_shift[None, None, :]
    )
    noisy = jnp.where(both_notes[:, :rows, None] == 1, mask_base[None], base[None]) * condition
    all_rows = jnp.concatenate([base[None], noisy], axis=0).astype(jnp.bfloat16)
    wide = jnp.dot(
        all_rows.reshape(streams * rows, -1), weights, preferred_element_type=jnp.float32
    )
    raw = wide[:, :q_width]
    key_wide = wide[:, q_width : q_width + HD]
    keys = (key_wide * inverse_rms(key_wide) * k_gain).astype(jnp.bfloat16)
    values = wide[:, q_width + HD :].astype(jnp.bfloat16)
    own = jnp.concatenate([keys, values], axis=1).reshape(streams, rows, 2 * HD)
    spans = lax.axis_size("ctx")
    attended = attend(raw, q_gain[None, :], own, streams, rows, heads, spans)
    attended = attended.reshape(streams, rows, q_width)
    kept = jnp.concatenate(
        [attended[:1], lax.dynamic_slice_in_dim(attended, 1 + mine, 1, axis=0)], axis=0
    )
    given = jnp.concatenate(
        [attended[:1], lax.dynamic_slice_in_dim(attended, 2 - mine, 1, axis=0)], axis=0
    )
    taken = lax.ppermute(given, "copy", SWAP)
    head_rows = ordered(kept, taken, 2).reshape(2 * rows, 2 * q_width)
    half = w_out.shape[1] // 2
    away = lax.dynamic_slice_in_dim(w_out, (1 - core) * half, half, axis=1)
    here = lax.dynamic_slice_in_dim(w_out, core * half, half, axis=1)
    sent = jnp.dot(head_rows, away, preferred_element_type=jnp.float32).astype(jnp.bfloat16)
    received = lax.ppermute(sent, "tp", SWAP)
    mixed = jnp.dot(head_rows, here, preferred_element_type=jnp.float32) + received.astype(
        jnp.float32
    )
    clean_out = mixed[:rows].astype(jnp.bfloat16)
    live_rows = jnp.repeat(block_live, BLK, axis=1).astype(jnp.float32)
    noised_out = (mixed[None, rows:] * live_rows[:, :, None]).astype(jnp.bfloat16)
    return (clean_out, noised_out)


def solution(mesh):
    in_specs = (
        P("ctx", "copy"),
        P(),
        P(),
        P(),
        P(None, "tp"),
        P(None, "tp"),
        P(None, "tp"),
        P("tp", None),
        P(),
        P(),
        P("copy", "ctx"),
        P("copy", "ctx"),
        P("copy"),
    )
    out_specs = (P("ctx", "tp"), P("copy", "ctx", "tp"))
    return jax.shard_map(
        on_device, mesh=mesh, in_specs=in_specs, out_specs=out_specs, check_vma=False
    )
```

```python
import functools
import math

import jax
import jax.numpy as jnp
from jax import lax
from jax.experimental import pallas as pl
from jax.experimental.pallas import tpu as pltpu
from jax.sharding import PartitionSpec as P

HD = 128
BLK = 64
TSTEPS = 1000
EPS = 1e-06
GROUP = 4
MESH = pl.DeviceIdType.MESH


def inverse_rms(values):
    return lax.rsqrt(jnp.mean(values * values, axis=-1, keepdims=True) + EPS)


def attend_kernel(
    rows, heads, streams, spans, raw_ref, gain_ref, own_ref, out_ref, kv_ref, q_ref, acc_ref, send_sem, recv_sem, forward_sem
):
    me = lax.axis_index("ctx")

    barrier = pltpu.get_barrier_semaphore()

    def greet(step, carry):
        pl.semaphore_signal(
            barrier, inc=1, device_id={"ctx": lax.rem(me + step, spans)}, device_id_type=MESH
        )
        return carry

    lax.fori_loop(1, spans, greet, 0)
    pl.semaphore_wait(barrier, spans - 1)

    def push(target):
        return pltpu.make_async_remote_copy(
            src_ref=own_ref.at[0],
            dst_ref=kv_ref.at[me],
            send_sem=send_sem.at[target],
            recv_sem=recv_sem.at[me],
            device_id={"ctx": target},
            device_id_type=MESH,
        )

    def arrival(source):
        return pltpu.make_async_remote_copy(
            src_ref=own_ref.at[0],
            dst_ref=kv_ref.at[source],
            send_sem=send_sem.at[source],
            recv_sem=recv_sem.at[source],
            device_id={"ctx": source},
            device_id_type=MESH,
        )

    pair = me // 2
    lane = lax.rem(me, 2)
    partner = me + 1 - 2 * lane

    def relayed(index):
        return lax.rem(index, 4) != 3

    def each_push(act):
        @pl.when(lane == 0)
        def _():
            act(push(partner))

        def to_pair(index, carry):
            act(push(2 * index + lane))

            @pl.when(jnp.logical_not(relayed(pair)))
            def _():
                act(push(2 * index + 1 - lane))

            return carry

        lax.fori_loop(pair + 1, spans // 2, to_pair, 0)

    def forward(index):
        slot = 2 * index + lane
        return pltpu.make_async_remote_copy(
            src_ref=kv_ref.at[slot],
            dst_ref=kv_ref.at[slot],
            send_sem=forward_sem.at[slot],
            recv_sem=recv_sem.at[slot],
            device_id={"ctx": partner},
            device_id_type=MESH,
        )

    def relay(step, carry):
        index = pair - 1 - step
        arrival(2 * index + lane).wait_recv()

        @pl.when(relayed(index))
        def _():
            forward(index).start()

        return carry

    def end_relay(index, carry):
        @pl.when(relayed(index))
        def _():
            forward(index).wait_send()

        return carry

    each_push(lambda copy: copy.start())
    scale = math.log2(math.e) / math.sqrt(HD)
    gain = gain_ref[...]
    query_block = lax.broadcasted_iota(jnp.int32, (rows, rows), 0) // BLK
    key_block = lax.broadcasted_iota(jnp.int32, (rows, rows), 1) // BLK

    def split(kv):
        ones = jnp.ones((kv.shape[0], HD), jnp.bfloat16)
        return kv[:, :HD], jnp.concatenate([kv[:, HD:], ones], axis=1)

    def exponentials(queries, keys):
        scores = lax.dot_general(
            queries, keys, (((1,), (1,)), ((), ())), preferred_element_type=jnp.float32
        )
        return jnp.exp2(scores * scale)

    keys, values = split(own_ref[0])
    for stream in range(streams):
        if stream:
            self_keys, self_values = split(own_ref[stream])
        for head in range(heads):
            raw = raw_ref[stream * rows : (stream + 1) * rows, head * HD : (head + 1) * HD]
            queries = (raw * inverse_rms(raw) * gain).astype(jnp.bfloat16)
            at = pl.ds((stream * heads + head) * rows, rows)
            q_ref[at] = queries
            allowed = key_block < query_block if stream else key_block <= query_block
            weights = jnp.where(allowed, exponentials(queries, keys), 0.0).astype(jnp.bfloat16)
            total = jnp.dot(weights, values, preferred_element_type=jnp.float32)
            if stream:
                weights = jnp.where(
                    key_block == query_block, exponentials(queries, self_keys), 0.0
                ).astype(jnp.bfloat16)
                total += jnp.dot(weights, self_values, preferred_element_type=jnp.float32)
            acc_ref[at] = total

    def accumulate(start, count):
        group_keys, group_values = split(kv_ref[pl.ds(start, count)].reshape(count * rows, 2 * HD))
        for tile in range(streams * heads):
            at = pl.ds(tile * rows, rows)
            weights = exponentials(q_ref[at], group_keys).astype(jnp.bfloat16)
            acc_ref[at] += jnp.dot(weights, group_values, preferred_element_type=jnp.float32)

    pairs = GROUP // 2

    def whole(step, carry):
        lax.fori_loop((step + 1) * pairs, jnp.minimum((step + 2) * pairs, pair), relay, 0)
        start = pair - (step + 1) * pairs
        for offset in range(pairs):
            arrival(2 * (start + offset) + 1 - lane).wait_recv()
        accumulate(2 * start, GROUP)
        return carry

    def last(step, carry):
        index = lax.rem(pair, pairs) - 1 - step
        arrival(2 * index + 1 - lane).wait_recv()
        accumulate(2 * index, 2)
        return carry

    lax.fori_loop(0, jnp.minimum(pairs, pair), relay, 0)

    @pl.when(lane == 1)
    def _():
        arrival(2 * pair).wait_recv()
        accumulate(2 * pair, 1)

    lax.fori_loop(0, pair // pairs, whole, 0)
    lax.fori_loop(0, lax.rem(pair, pairs), last, 0)
    for stream in range(streams):
        for head in range(heads):
            at = pl.ds((stream * heads + head) * rows, rows)
            out_ref[stream * rows : (stream + 1) * rows, head * HD : (head + 1) * HD] = (
                acc_ref[at, :HD] / acc_ref[at, HD:]
            ).astype(jnp.bfloat16)
    each_push(lambda copy: copy.wait_send())
    lax.fori_loop(0, pair, end_relay, 0)


def attend(raw, q_gain, own, streams, rows, heads, spans):
    return pl.pallas_call(
        functools.partial(attend_kernel, rows, heads, streams, spans),
        out_shape=jax.ShapeDtypeStruct((streams * rows, heads * HD), jnp.bfloat16),
        in_specs=[pl.BlockSpec(memory_space=pltpu.VMEM)] * 3,
        out_specs=pl.BlockSpec(memory_space=pltpu.VMEM),
        scratch_shapes=[
            pltpu.VMEM((spans, rows, 2 * HD), jnp.bfloat16),
            pltpu.VMEM((streams * heads * rows, HD), jnp.bfloat16),
            pltpu.VMEM((streams * heads * rows, 2 * HD), jnp.float32),
            pltpu.SemaphoreType.DMA((spans,)),
            pltpu.SemaphoreType.DMA((spans,)),
            pltpu.SemaphoreType.DMA((spans,)),
        ],
        compiler_params=pltpu.CompilerParams(
            vmem_limit_bytes=48 * 2**20, collective_id=0, has_side_effects=True
        ),
    )(raw, q_gain, own)


SWAP = [(0, 1), (1, 0)]


def on_device(
    clean_tokens,
    norm_gain,
    mask_embed,
    time_shift,
    w_query,
    w_key,
    w_value,
    w_out,
    q_gain,
    k_gain,
    masked,
    block_live,
    timesteps,
):
    mine = lax.axis_index("copy")
    core = lax.axis_index("tp")
    first = mine == 0
    rows = clean_tokens.shape[0]
    streams = 3
    q_width = w_query.shape[1] // 2
    heads = q_width // HD

    def ordered(own, other, axis):
        return jnp.where(
            first,
            jnp.concatenate([own, other], axis=axis),
            jnp.concatenate([other, own], axis=axis),
        )

    notes = jnp.concatenate([masked, timesteps[:, None]], axis=1)
    other_notes = lax.ppermute(notes, "copy", SWAP)
    other_tokens = lax.ppermute(clean_tokens, "copy", SWAP)
    weights = jnp.concatenate(
        [
            lax.dynamic_slice_in_dim(w_query, mine * q_width, q_width, axis=1),
            lax.dynamic_slice_in_dim(w_key, mine * HD, HD, axis=1),
            lax.dynamic_slice_in_dim(w_value, mine * HD, HD, axis=1),
        ],
        axis=1,
    )
    features = ordered(clean_tokens, other_tokens, 1).astype(jnp.float32)
    both_notes = ordered(notes, other_notes, 0)
    gain = norm_gain.astype(jnp.float32)
    base = features * inverse_rms(features) * gain
    mask_wide = mask_embed.astype(jnp.float32)[None, :]
    mask_base = mask_wide * inverse_rms(mask_wide) * gain
    condition = (
        1.0 + both_notes[:, rows:].astype(jnp.float32)[:, :, None] / TSTEPS * time_shift[None, None, :]
    )
    noisy = jnp.where(both_notes[:, :rows, None] == 1, mask_base[None], base[None]) * condition
    all_rows = jnp.concatenate([base[None], noisy], axis=0).astype(jnp.bfloat16)
    wide = jnp.dot(
        all_rows.reshape(streams * rows, -1), weights, preferred_element_type=jnp.float32
    )
    raw = wide[:, :q_width]
    key_wide = wide[:, q_width : q_width + HD]
    keys = (key_wide * inverse_rms(key_wide) * k_gain).astype(jnp.bfloat16)
    values = wide[:, q_width + HD :].astype(jnp.bfloat16)
    own = jnp.concatenate([keys, values], axis=1).reshape(streams, rows, 2 * HD)
    spans = lax.axis_size("ctx")
    attended = attend(raw, q_gain[None, :], own, streams, rows, heads, spans)
    attended = attended.reshape(streams, rows, q_width)
    kept = jnp.concatenate(
        [attended[:1], lax.dynamic_slice_in_dim(attended, 1 + mine, 1, axis=0)], axis=0
    )
    given = jnp.concatenate(
        [attended[:1], lax.dynamic_slice_in_dim(attended, 2 - mine, 1, axis=0)], axis=0
    )
    taken = lax.ppermute(given, "copy", SWAP)
    head_rows = ordered(kept, taken, 2).reshape(2 * rows, 2 * q_width)
    half = w_out.shape[1] // 2
    away = lax.dynamic_slice_in_dim(w_out, (1 - core) * half, half, axis=1)
    here = lax.dynamic_slice_in_dim(w_out, core * half, half, axis=1)
    sent = jnp.dot(head_rows, away, preferred_element_type=jnp.float32).astype(jnp.bfloat16)
    received = lax.ppermute(sent, "tp", SWAP)
    mixed = jnp.dot(head_rows, here, preferred_element_type=jnp.float32) + received.astype(
        jnp.float32
    )
    clean_out = mixed[:rows].astype(jnp.bfloat16)
    live_rows = jnp.repeat(block_live, BLK, axis=1).astype(jnp.float32)
    noised_out = (mixed[None, rows:] * live_rows[:, :, None]).astype(jnp.bfloat16)
    return (clean_out, noised_out)


def solution(mesh):
    in_specs = (
        P("ctx", "copy"),
        P(),
        P(),
        P(),
        P(None, "tp"),
        P(None, "tp"),
        P(None, "tp"),
        P("tp", None),
        P(),
        P(),
        P("copy", "ctx"),
        P("copy", "ctx"),
        P("copy"),
    )
    out_specs = (P("ctx", "tp"), P("copy", "ctx", "tp"))
    return jax.shard_map(
        on_device, mesh=mesh, in_specs=in_specs, out_specs=out_specs, check_vma=False
    )
```

```python
import functools
import math

import jax
import jax.numpy as jnp
from jax import lax
from jax.experimental import pallas as pl
from jax.experimental.pallas import tpu as pltpu
from jax.sharding import PartitionSpec as P

HD = 128
BLK = 64
TSTEPS = 1000
EPS = 1e-06
GROUP = 4
MESH = pl.DeviceIdType.MESH


def inverse_rms(values):
    return lax.rsqrt(jnp.mean(values * values, axis=-1, keepdims=True) + EPS)


def attend_kernel(
    rows, heads, streams, spans, raw_ref, gain_ref, own_ref, out_ref, kv_ref, q_ref, acc_ref, send_sem, recv_sem, forward_sem
):
    me = lax.axis_index("ctx")

    barrier = pltpu.get_barrier_semaphore()

    def greet(step, carry):
        pl.semaphore_signal(
            barrier, inc=1, device_id={"ctx": lax.rem(me + step, spans)}, device_id_type=MESH
        )
        return carry

    lax.fori_loop(1, spans, greet, 0)
    pl.semaphore_wait(barrier, spans - 1)

    def push(target):
        return pltpu.make_async_remote_copy(
            src_ref=own_ref.at[0],
            dst_ref=kv_ref.at[me],
            send_sem=send_sem.at[target],
            recv_sem=recv_sem.at[me],
            device_id={"ctx": target},
            device_id_type=MESH,
        )

    def arrival(source):
        return pltpu.make_async_remote_copy(
            src_ref=own_ref.at[0],
            dst_ref=kv_ref.at[source],
            send_sem=send_sem.at[source],
            recv_sem=recv_sem.at[source],
            device_id={"ctx": source},
            device_id_type=MESH,
        )

    pair = me // 2
    lane = lax.rem(me, 2)
    partner = me + 1 - 2 * lane

    def relayed(index):
        return lax.rem(index, 4) != 3

    def each_push(act):
        @pl.when(lane == 0)
        def _():
            act(push(partner))

        def to_pair(index, carry):
            act(push(2 * index + lane))

            @pl.when(jnp.logical_not(relayed(pair)))
            def _():
                act(push(2 * index + 1 - lane))

            return carry

        lax.fori_loop(pair + 1, spans // 2, to_pair, 0)

    def forward(index):
        slot = 2 * index + lane
        return pltpu.make_async_remote_copy(
            src_ref=kv_ref.at[slot],
            dst_ref=kv_ref.at[slot],
            send_sem=forward_sem.at[slot],
            recv_sem=recv_sem.at[slot],
            device_id={"ctx": partner},
            device_id_type=MESH,
        )

    def relay(step, carry):
        index = pair - 1 - step
        arrival(2 * index + lane).wait_recv()

        @pl.when(relayed(index))
        def _():
            forward(index).start()

        return carry

    def end_relay(index, carry):
        @pl.when(relayed(index))
        def _():
            forward(index).wait_send()

        return carry

    each_push(lambda copy: copy.start())
    scale = math.log2(math.e) / math.sqrt(HD)
    gain = gain_ref[...]
    query_block = lax.broadcasted_iota(jnp.int32, (rows, rows), 0) // BLK
    key_block = lax.broadcasted_iota(jnp.int32, (rows, rows), 1) // BLK

    def split(kv):
        ones = jnp.ones((kv.shape[0], HD), jnp.bfloat16)
        return kv[:, :HD], jnp.concatenate([kv[:, HD:], ones], axis=1)

    def exponentials(queries, keys):
        scores = lax.dot_general(
            queries, keys, (((1,), (1,)), ((), ())), preferred_element_type=jnp.float32
        )
        return jnp.exp2(scores * scale)

    keys, values = split(own_ref[0])
    for stream in range(streams):
        if stream:
            self_keys, self_values = split(own_ref[stream])
        for head in range(heads):
            raw = raw_ref[stream * rows : (stream + 1) * rows, head * HD : (head + 1) * HD]
            queries = (raw * inverse_rms(raw) * gain).astype(jnp.bfloat16)
            at = pl.ds((stream * heads + head) * rows, rows)
            q_ref[at] = queries
            allowed = key_block < query_block if stream else key_block <= query_block
            weights = jnp.where(allowed, exponentials(queries, keys), 0.0).astype(jnp.bfloat16)
            total = jnp.dot(weights, values, preferred_element_type=jnp.float32)
            if stream:
                weights = jnp.where(
                    key_block == query_block, exponentials(queries, self_keys), 0.0
                ).astype(jnp.bfloat16)
                total += jnp.dot(weights, self_values, preferred_element_type=jnp.float32)
            acc_ref[at] = total

    def accumulate(start, count):
        group_keys, group_values = split(kv_ref[pl.ds(start, count)].reshape(count * rows, 2 * HD))
        for tile in range(streams * heads):
            at = pl.ds(tile * rows, rows)
            weights = exponentials(q_ref[at], group_keys).astype(jnp.bfloat16)
            acc_ref[at] += jnp.dot(weights, group_values, preferred_element_type=jnp.float32)

    pairs = GROUP // 2

    def whole(step, carry):
        lax.fori_loop((step + 1) * pairs, jnp.minimum((step + 2) * pairs, pair), relay, 0)
        start = pair - (step + 1) * pairs
        for offset in range(pairs):
            arrival(2 * (start + offset) + 1 - lane).wait_recv()
        accumulate(2 * start, GROUP)
        return carry

    def last(step, carry):
        index = lax.rem(pair, pairs) - 1 - step
        arrival(2 * index + 1 - lane).wait_recv()
        accumulate(2 * index, 2)
        return carry

    lax.fori_loop(0, jnp.minimum(pairs, pair), relay, 0)

    @pl.when(lane == 1)
    def _():
        arrival(2 * pair).wait_recv()
        accumulate(2 * pair, 1)

    lax.fori_loop(0, pair // pairs, whole, 0)
    lax.fori_loop(0, lax.rem(pair, pairs), last, 0)
    for stream in range(streams):
        for head in range(heads):
            at = pl.ds((stream * heads + head) * rows, rows)
            out_ref[stream * rows : (stream + 1) * rows, head * HD : (head + 1) * HD] = (
                acc_ref[at, :HD] / acc_ref[at, HD:]
            ).astype(jnp.bfloat16)
    each_push(lambda copy: copy.wait_send())
    lax.fori_loop(0, pair, end_relay, 0)


def attend(raw, q_gain, own, streams, rows, heads, spans):
    return pl.pallas_call(
        functools.partial(attend_kernel, rows, heads, streams, spans),
        out_shape=jax.ShapeDtypeStruct((streams * rows, heads * HD), jnp.bfloat16),
        in_specs=[pl.BlockSpec(memory_space=pltpu.VMEM)] * 3,
        out_specs=pl.BlockSpec(memory_space=pltpu.VMEM),
        scratch_shapes=[
            pltpu.VMEM((spans, rows, 2 * HD), jnp.bfloat16),
            pltpu.VMEM((streams * heads * rows, HD), jnp.bfloat16),
            pltpu.VMEM((streams * heads * rows, 2 * HD), jnp.float32),
            pltpu.SemaphoreType.DMA((spans,)),
            pltpu.SemaphoreType.DMA((spans,)),
            pltpu.SemaphoreType.DMA((spans,)),
        ],
        compiler_params=pltpu.CompilerParams(
            vmem_limit_bytes=48 * 2**20, collective_id=0, has_side_effects=True
        ),
    )(raw, q_gain, own)


SWAP = [(0, 1), (1, 0)]


def on_device(
    clean_tokens,
    norm_gain,
    mask_embed,
    time_shift,
    w_query,
    w_key,
    w_value,
    w_out,
    q_gain,
    k_gain,
    masked,
    block_live,
    timesteps,
):
    mine = lax.axis_index("copy")
    core = lax.axis_index("tp")
    first = mine == 0
    rows = clean_tokens.shape[0]
    streams = 3
    q_width = w_query.shape[1] // 2
    heads = q_width // HD

    def ordered(own, other, axis):
        return jnp.where(
            first,
            jnp.concatenate([own, other], axis=axis),
            jnp.concatenate([other, own], axis=axis),
        )

    notes = jnp.concatenate([masked, timesteps[:, None]], axis=1)
    other_notes = lax.ppermute(notes, "copy", SWAP)
    near_rows = lax.ppermute(
        lax.dynamic_slice_in_dim(clean_tokens, core * (rows // 2), rows // 2, axis=0), "copy", SWAP
    )
    far_rows = lax.ppermute(near_rows, "tp", SWAP)
    other_tokens = jnp.where(
        core == 0,
        jnp.concatenate([near_rows, far_rows], axis=0),
        jnp.concatenate([far_rows, near_rows], axis=0),
    )
    weights = jnp.concatenate(
        [
            lax.dynamic_slice_in_dim(w_query, mine * q_width, q_width, axis=1),
            lax.dynamic_slice_in_dim(w_key, mine * HD, HD, axis=1),
            lax.dynamic_slice_in_dim(w_value, mine * HD, HD, axis=1),
        ],
        axis=1,
    )
    features = ordered(clean_tokens, other_tokens, 1).astype(jnp.float32)
    both_notes = ordered(notes, other_notes, 0)
    gain = norm_gain.astype(jnp.float32)
    base = features * inverse_rms(features) * gain
    mask_wide = mask_embed.astype(jnp.float32)[None, :]
    mask_base = mask_wide * inverse_rms(mask_wide) * gain
    condition = (
        1.0 + both_notes[:, rows:].astype(jnp.float32)[:, :, None] / TSTEPS * time_shift[None, None, :]
    )
    noisy = jnp.where(both_notes[:, :rows, None] == 1, mask_base[None], base[None]) * condition
    all_rows = jnp.concatenate([base[None], noisy], axis=0).astype(jnp.bfloat16)
    wide = jnp.dot(
        all_rows.reshape(streams * rows, -1), weights, preferred_element_type=jnp.float32
    )
    raw = wide[:, :q_width]
    key_wide = wide[:, q_width : q_width + HD]
    keys = (key_wide * inverse_rms(key_wide) * k_gain).astype(jnp.bfloat16)
    values = wide[:, q_width + HD :].astype(jnp.bfloat16)
    own = jnp.concatenate([keys, values], axis=1).reshape(streams, rows, 2 * HD)
    spans = lax.axis_size("ctx")
    attended = attend(raw, q_gain[None, :], own, streams, rows, heads, spans)
    attended = attended.reshape(streams, rows, q_width)
    taken_clean = lax.ppermute(attended[0], "copy", SWAP)
    taken_noised = lax.ppermute(
        lax.dynamic_index_in_dim(attended, 2 - mine, axis=0, keepdims=False), "copy", SWAP
    )
    kept_noised = lax.dynamic_index_in_dim(attended, 1 + mine, axis=0, keepdims=False)
    half = w_out.shape[1] // 2
    away = lax.dynamic_slice_in_dim(w_out, (1 - core) * half, half, axis=1)
    here = lax.dynamic_slice_in_dim(w_out, core * half, half, axis=1)

    def partial(head_rows, weight):
        return jnp.dot(head_rows, weight, preferred_element_type=jnp.float32)

    clean_rows = ordered(attended[0], taken_clean, 1)
    clean_sent = partial(clean_rows, away).astype(jnp.bfloat16)
    clean_received = lax.ppermute(clean_sent, "tp", SWAP)
    noised_rows = ordered(kept_noised, taken_noised, 1)
    noised_sent = partial(noised_rows, away).astype(jnp.bfloat16)
    noised_received = lax.ppermute(noised_sent, "tp", SWAP)
    clean_out = (partial(clean_rows, here) + clean_received.astype(jnp.float32)).astype(jnp.bfloat16)
    mixed = partial(noised_rows, here) + noised_received.astype(jnp.float32)
    live_rows = jnp.repeat(block_live, BLK, axis=1).astype(jnp.float32)
    noised_out = (mixed[None] * live_rows[:, :, None]).astype(jnp.bfloat16)
    return (clean_out, noised_out)


def solution(mesh):
    in_specs = (
        P("ctx", "copy"),
        P(),
        P(),
        P(),
        P(None, "tp"),
        P(None, "tp"),
        P(None, "tp"),
        P("tp", None),
        P(),
        P(),
        P("copy", "ctx"),
        P("copy", "ctx"),
        P("copy"),
    )
    out_specs = (P("ctx", "tp"), P("copy", "ctx", "tp"))
    return jax.shard_map(
        on_device, mesh=mesh, in_specs=in_specs, out_specs=out_specs, check_vma=False
    )
```

```python
import functools
import math

import jax
import jax.numpy as jnp
from jax import lax
from jax.experimental import pallas as pl
from jax.experimental.pallas import tpu as pltpu
from jax.sharding import PartitionSpec as P

HD = 128
BLK = 64
TSTEPS = 1000
EPS = 1e-06
GROUP = 4
MESH = pl.DeviceIdType.MESH


def inverse_rms(values):
    return lax.rsqrt(jnp.mean(values * values, axis=-1, keepdims=True) + EPS)


def attend_kernel(
    rows, heads, streams, spans, raw_ref, gain_ref, own_ref, out_ref, kv_ref, q_ref, acc_ref, send_sem, recv_sem, forward_sem
):
    me = lax.axis_index("ctx")

    barrier = pltpu.get_barrier_semaphore()

    def greet(step, carry):
        pl.semaphore_signal(
            barrier, inc=1, device_id={"ctx": lax.rem(me + step, spans)}, device_id_type=MESH
        )
        return carry

    lax.fori_loop(1, spans, greet, 0)
    pl.semaphore_wait(barrier, spans - 1)

    def push(target):
        return pltpu.make_async_remote_copy(
            src_ref=own_ref.at[0],
            dst_ref=kv_ref.at[me],
            send_sem=send_sem.at[target],
            recv_sem=recv_sem.at[me],
            device_id={"ctx": target},
            device_id_type=MESH,
        )

    def arrival(source):
        return pltpu.make_async_remote_copy(
            src_ref=own_ref.at[0],
            dst_ref=kv_ref.at[source],
            send_sem=send_sem.at[source],
            recv_sem=recv_sem.at[source],
            device_id={"ctx": source},
            device_id_type=MESH,
        )

    pair = me // 2
    lane = lax.rem(me, 2)
    partner = me + 1 - 2 * lane

    def relayed(index):
        return lax.rem(index, 4) != 3

    def each_push(act):
        @pl.when(lane == 0)
        def _():
            act(push(partner))

        def to_pair(index, carry):
            act(push(2 * index + lane))

            @pl.when(jnp.logical_not(relayed(pair)))
            def _():
                act(push(2 * index + 1 - lane))

            return carry

        lax.fori_loop(pair + 1, spans // 2, to_pair, 0)

    def forward(index):
        slot = 2 * index + lane
        return pltpu.make_async_remote_copy(
            src_ref=kv_ref.at[slot],
            dst_ref=kv_ref.at[slot],
            send_sem=forward_sem.at[slot],
            recv_sem=recv_sem.at[slot],
            device_id={"ctx": partner},
            device_id_type=MESH,
        )

    def relay(step, carry):
        index = pair - 1 - step
        arrival(2 * index + lane).wait_recv()

        @pl.when(relayed(index))
        def _():
            forward(index).start()

        return carry

    def end_relay(index, carry):
        @pl.when(relayed(index))
        def _():
            forward(index).wait_send()

        return carry

    each_push(lambda copy: copy.start())
    scale = math.log2(math.e) / math.sqrt(HD)
    gain = gain_ref[...]
    query_block = lax.broadcasted_iota(jnp.int32, (rows, rows), 0) // BLK
    key_block = lax.broadcasted_iota(jnp.int32, (rows, rows), 1) // BLK

    def split(kv):
        ones = jnp.ones((kv.shape[0], HD), jnp.bfloat16)
        return kv[:, :HD], jnp.concatenate([kv[:, HD:], ones], axis=1)

    def exponentials(queries, keys):
        scores = lax.dot_general(
            queries, keys, (((1,), (1,)), ((), ())), preferred_element_type=jnp.float32
        )
        return jnp.exp2(scores * scale)

    keys, values = split(own_ref[0])
    for stream in range(streams):
        if stream:
            self_keys, self_values = split(own_ref[stream])
        for head in range(heads):
            raw = raw_ref[stream * rows : (stream + 1) * rows, head * HD : (head + 1) * HD]
            queries = (raw * inverse_rms(raw) * gain).astype(jnp.bfloat16)
            at = pl.ds((stream * heads + head) * rows, rows)
            q_ref[at] = queries
            allowed = key_block < query_block if stream else key_block <= query_block
            weights = jnp.where(allowed, exponentials(queries, keys), 0.0).astype(jnp.bfloat16)
            total = jnp.dot(weights, values, preferred_element_type=jnp.float32)
            if stream:
                weights = jnp.where(
                    key_block == query_block, exponentials(queries, self_keys), 0.0
                ).astype(jnp.bfloat16)
                total += jnp.dot(weights, self_values, preferred_element_type=jnp.float32)
            acc_ref[at] = total

    def accumulate(start, count):
        group_keys, group_values = split(kv_ref[pl.ds(start, count)].reshape(count * rows, 2 * HD))
        for tile in range(streams * heads):
            at = pl.ds(tile * rows, rows)
            weights = exponentials(q_ref[at], group_keys).astype(jnp.bfloat16)
            acc_ref[at] += jnp.dot(weights, group_values, preferred_element_type=jnp.float32)

    pairs = GROUP // 2

    def whole(step, carry):
        lax.fori_loop((step + 1) * pairs, jnp.minimum((step + 2) * pairs, pair), relay, 0)
        start = pair - (step + 1) * pairs
        for offset in range(pairs):
            arrival(2 * (start + offset) + 1 - lane).wait_recv()
        accumulate(2 * start, GROUP)
        return carry

    def last(step, carry):
        index = lax.rem(pair, pairs) - 1 - step
        arrival(2 * index + 1 - lane).wait_recv()
        accumulate(2 * index, 2)
        return carry

    lax.fori_loop(0, jnp.minimum(pairs, pair), relay, 0)

    @pl.when(lane == 1)
    def _():
        arrival(2 * pair).wait_recv()
        accumulate(2 * pair, 1)

    lax.fori_loop(0, pair // pairs, whole, 0)
    lax.fori_loop(0, lax.rem(pair, pairs), last, 0)
    for stream in range(streams):
        for head in range(heads):
            at = pl.ds((stream * heads + head) * rows, rows)
            out_ref[stream * rows : (stream + 1) * rows, head * HD : (head + 1) * HD] = (
                acc_ref[at, :HD] / acc_ref[at, HD:]
            ).astype(jnp.bfloat16)
    each_push(lambda copy: copy.wait_send())
    lax.fori_loop(0, pair, end_relay, 0)


def attend(raw, q_gain, own, streams, rows, heads, spans):
    return pl.pallas_call(
        functools.partial(attend_kernel, rows, heads, streams, spans),
        out_shape=jax.ShapeDtypeStruct((streams * rows, heads * HD), jnp.bfloat16),
        in_specs=[pl.BlockSpec(memory_space=pltpu.VMEM)] * 3,
        out_specs=pl.BlockSpec(memory_space=pltpu.VMEM),
        scratch_shapes=[
            pltpu.VMEM((spans, rows, 2 * HD), jnp.bfloat16),
            pltpu.VMEM((streams * heads * rows, HD), jnp.bfloat16),
            pltpu.VMEM((streams * heads * rows, 2 * HD), jnp.float32),
            pltpu.SemaphoreType.DMA((spans,)),
            pltpu.SemaphoreType.DMA((spans,)),
            pltpu.SemaphoreType.DMA((spans,)),
        ],
        compiler_params=pltpu.CompilerParams(
            vmem_limit_bytes=48 * 2**20, collective_id=0, has_side_effects=True
        ),
    )(raw, q_gain, own)


def project_kernel(
    rows, att_ref, w_out_ref, live_ref, clean_ref, noised_ref,
    weight_ref, taken_ref, away_ref, here_ref, sent_ref, got_ref, give_sem, take_sem, send_sem, recv_sem, load_sem,
):
    mine = lax.axis_index("copy")
    core = lax.axis_index("tp")
    depth = att_ref.shape[1]
    loads = []
    for number, owner in enumerate((mine, 1 - mine)):
        at = pl.ds(pl.multiple_of(owner * depth, depth), depth)
        load = pltpu.make_async_copy(w_out_ref.at[at], weight_ref.at[at], load_sem.at[number])
        load.start()
        loads.append(load)
    barrier = pltpu.get_barrier_semaphore()
    pl.semaphore_signal(barrier, inc=1, device_id={"copy": 1 - mine}, device_id_type=MESH)
    pl.semaphore_signal(barrier, inc=1, device_id={"tp": 1 - core}, device_id_type=MESH)
    pl.semaphore_wait(barrier, 2)

    pieces, _, width = sent_ref.shape

    def part(start):
        return pl.ds(pl.multiple_of(start, rows), rows)

    gifts = [
        pltpu.make_async_remote_copy(
            src_ref=att_ref.at[part(start)],
            dst_ref=taken_ref.at[pl.ds(number * rows, rows)],
            send_sem=give_sem.at[number],
            recv_sem=take_sem.at[number],
            device_id={"copy": 1 - mine},
            device_id_type=MESH,
        )
        for number, start in enumerate((0, (2 - mine) * rows))
    ]
    for gift in gifts:
        gift.start()

    def weight(half, owner, piece):
        return weight_ref[
            pl.ds(pl.multiple_of(owner * depth, depth), depth),
            pl.ds(pl.multiple_of((half * pieces + piece) * width, width), width),
        ]

    def product(values, half, owner, piece):
        return jnp.dot(values, weight(half, owner, piece), preferred_element_type=jnp.float32)

    kept = jnp.concatenate([att_ref[:rows], att_ref[part((1 + mine) * rows)]], axis=0)
    loads[0].wait()
    for piece in range(pieces):
        away_ref[piece] = product(kept, 1 - core, mine, piece)
    for piece in range(pieces):
        here_ref[piece] = product(kept, core, mine, piece)
    for gift in gifts:
        gift.wait_recv()
    loads[1].wait()
    taken = taken_ref[...]
    copies = []
    for piece in range(pieces):
        sent_ref[piece] = (away_ref[piece] + product(taken, 1 - core, 1 - mine, piece)).astype(jnp.bfloat16)
        copy = pltpu.make_async_remote_copy(
            src_ref=sent_ref.at[piece],
            dst_ref=got_ref.at[piece],
            send_sem=send_sem.at[piece],
            recv_sem=recv_sem.at[piece],
            device_id={"tp": 1 - core},
            device_id_type=MESH,
        )
        copy.start()
        copies.append(copy)
    for piece in range(pieces):
        here_ref[piece] += product(taken, core, 1 - mine, piece)
    for piece, copy in enumerate(copies):
        copy.wait_recv()
        total = here_ref[piece] + got_ref[piece].astype(jnp.float32)
        at = pl.ds(piece * width, width)
        clean_ref[:, at] = total[:rows].astype(jnp.bfloat16)
        noised_ref[:, at] = (total[rows:] * live_ref[...]).astype(jnp.bfloat16)
    for copy in gifts + copies:
        copy.wait_send()


def project(attended, w_out, live_rows):
    rows = live_rows.shape[0]
    half = w_out.shape[1] // 2
    pieces = 4
    width = half // pieces
    out = jax.ShapeDtypeStruct((rows, half), jnp.bfloat16)
    return pl.pallas_call(
        functools.partial(project_kernel, rows),
        out_shape=(out, out),
        in_specs=[
            pl.BlockSpec(memory_space=pltpu.VMEM),
            pl.BlockSpec(memory_space=pltpu.HBM),
            pl.BlockSpec(memory_space=pltpu.VMEM),
        ],
        out_specs=(pl.BlockSpec(memory_space=pltpu.VMEM),) * 2,
        scratch_shapes=[
            pltpu.VMEM(w_out.shape, jnp.bfloat16),
            pltpu.VMEM((2 * rows, attended.shape[1]), jnp.bfloat16),
            pltpu.VMEM((pieces, 2 * rows, width), jnp.float32),
            pltpu.VMEM((pieces, 2 * rows, width), jnp.float32),
            pltpu.VMEM((pieces, 2 * rows, width), jnp.bfloat16),
            pltpu.VMEM((pieces, 2 * rows, width), jnp.bfloat16),
            pltpu.SemaphoreType.DMA((2,)),
            pltpu.SemaphoreType.DMA((2,)),
            pltpu.SemaphoreType.DMA((pieces,)),
            pltpu.SemaphoreType.DMA((pieces,)),
            pltpu.SemaphoreType.DMA((2,)),
        ],
        compiler_params=pltpu.CompilerParams(
            vmem_limit_bytes=44 * 2**20, collective_id=1, has_side_effects=True
        ),
    )(attended, w_out, live_rows)


SWAP = [(0, 1), (1, 0)]


def on_device(
    clean_tokens,
    norm_gain,
    mask_embed,
    time_shift,
    w_query,
    w_key,
    w_value,
    w_out,
    q_gain,
    k_gain,
    masked,
    block_live,
    timesteps,
):
    mine = lax.axis_index("copy")
    core = lax.axis_index("tp")
    first = mine == 0
    rows = clean_tokens.shape[0]
    streams = 3
    q_width = w_query.shape[1] // 2
    heads = q_width // HD

    def ordered(own, other, axis):
        return jnp.where(
            first,
            jnp.concatenate([own, other], axis=axis),
            jnp.concatenate([other, own], axis=axis),
        )

    notes = jnp.concatenate([masked, timesteps[:, None]], axis=1)
    other_notes = lax.ppermute(notes, "copy", SWAP)
    near_rows = lax.ppermute(
        lax.dynamic_slice_in_dim(clean_tokens, core * (rows // 2), rows // 2, axis=0), "copy", SWAP
    )
    far_rows = lax.ppermute(near_rows, "tp", SWAP)
    other_tokens = jnp.where(
        core == 0,
        jnp.concatenate([near_rows, far_rows], axis=0),
        jnp.concatenate([far_rows, near_rows], axis=0),
    )
    weights = jnp.concatenate(
        [
            lax.dynamic_slice_in_dim(w_query, mine * q_width, q_width, axis=1),
            lax.dynamic_slice_in_dim(w_key, mine * HD, HD, axis=1),
            lax.dynamic_slice_in_dim(w_value, mine * HD, HD, axis=1),
        ],
        axis=1,
    )
    features = ordered(clean_tokens, other_tokens, 1).astype(jnp.float32)
    both_notes = ordered(notes, other_notes, 0)
    gain = norm_gain.astype(jnp.float32)
    base = features * inverse_rms(features) * gain
    mask_wide = mask_embed.astype(jnp.float32)[None, :]
    mask_base = mask_wide * inverse_rms(mask_wide) * gain
    condition = (
        1.0 + both_notes[:, rows:].astype(jnp.float32)[:, :, None] / TSTEPS * time_shift[None, None, :]
    )
    noisy = jnp.where(both_notes[:, :rows, None] == 1, mask_base[None], base[None]) * condition
    all_rows = jnp.concatenate([base[None], noisy], axis=0).astype(jnp.bfloat16)
    wide = jnp.dot(
        all_rows.reshape(streams * rows, -1), weights, preferred_element_type=jnp.float32
    )
    raw = wide[:, :q_width]
    key_wide = wide[:, q_width : q_width + HD]
    keys = (key_wide * inverse_rms(key_wide) * k_gain).astype(jnp.bfloat16)
    values = wide[:, q_width + HD :].astype(jnp.bfloat16)
    own = jnp.concatenate([keys, values], axis=1).reshape(streams, rows, 2 * HD)
    spans = lax.axis_size("ctx")
    attended = attend(raw, q_gain[None, :], own, streams, rows, heads, spans)
    live_rows = jnp.repeat(block_live[0], BLK)[:, None].astype(jnp.float32)
    clean_out, noised_out = project(attended, w_out, live_rows)
    noised_out = noised_out[None]
    return (clean_out, noised_out)


def solution(mesh):
    in_specs = (
        P("ctx", "copy"),
        P(),
        P(),
        P(),
        P(None, "tp"),
        P(None, "tp"),
        P(None, "tp"),
        P("tp", None),
        P(),
        P(),
        P("copy", "ctx"),
        P("copy", "ctx"),
        P("copy"),
    )
    out_specs = (P("ctx", "tp"), P("copy", "ctx", "tp"))
    return jax.shard_map(
        on_device, mesh=mesh, in_specs=in_specs, out_specs=out_specs, check_vma=False
    )
```

```python
import functools
import math

import jax
import jax.numpy as jnp
from jax import lax
from jax.experimental import pallas as pl
from jax.experimental.pallas import tpu as pltpu
from jax.sharding import PartitionSpec as P

HD = 128
BLK = 64
TSTEPS = 1000
EPS = 1e-06
GROUP = 4
SIDE = 4
MESH = pl.DeviceIdType.MESH


def inverse_rms(values):
    return lax.rsqrt(jnp.mean(values * values, axis=-1, keepdims=True) + EPS)


def attend_kernel(
    rows, heads, streams, spans, raw_ref, gain_ref, own_ref, out_ref, kv_ref, q_ref, acc_ref, send_sem, recv_sem, forward_sem
):
    me = lax.axis_index("ctx")

    barrier = pltpu.get_barrier_semaphore()

    def greet(step, carry):
        pl.semaphore_signal(
            barrier, inc=1, device_id={"ctx": lax.rem(me + step, spans)}, device_id_type=MESH
        )
        return carry

    lax.fori_loop(1, spans, greet, 0)
    pl.semaphore_wait(barrier, spans - 1)

    def push(target):
        return pltpu.make_async_remote_copy(
            src_ref=own_ref.at[0],
            dst_ref=kv_ref.at[me],
            send_sem=send_sem.at[target],
            recv_sem=recv_sem.at[me],
            device_id={"ctx": target},
            device_id_type=MESH,
        )

    def arrival(source):
        return pltpu.make_async_remote_copy(
            src_ref=own_ref.at[0],
            dst_ref=kv_ref.at[source],
            send_sem=send_sem.at[source],
            recv_sem=recv_sem.at[source],
            device_id={"ctx": source},
            device_id_type=MESH,
        )

    pair = me // 2
    lane = lax.rem(me, 2)
    partner = me + 1 - 2 * lane

    def relayed(index):
        return lax.rem(index, 4) != 3

    def each_push(act):
        @pl.when(lane == 0)
        def _():
            act(push(partner))

        def to_pair(step, carry):
            index = SIDE * (SIDE - 1 - step // SIDE) + lax.rem(pair + 1 + lax.rem(step, SIDE), SIDE)

            @pl.when(index > pair)
            def _():
                act(push(2 * index + lane))

            @pl.when(jnp.logical_and(index > pair, jnp.logical_not(relayed(pair))))
            def _():
                act(push(2 * index + 1 - lane))

            return carry

        lax.fori_loop(0, SIDE * SIDE, to_pair, 0)

    def forward(index):
        slot = 2 * index + lane
        return pltpu.make_async_remote_copy(
            src_ref=kv_ref.at[slot],
            dst_ref=kv_ref.at[slot],
            send_sem=forward_sem.at[slot],
            recv_sem=recv_sem.at[slot],
            device_id={"ctx": partner},
            device_id_type=MESH,
        )

    def relay(step, carry):
        index = pair - 1 - step
        arrival(2 * index + lane).wait_recv()

        @pl.when(relayed(index))
        def _():
            forward(index).start()

        return carry

    def end_relay(index, carry):
        @pl.when(relayed(index))
        def _():
            forward(index).wait_send()

        return carry

    each_push(lambda copy: copy.start())
    scale = math.log2(math.e) / math.sqrt(HD)
    gain = gain_ref[...]
    query_block = lax.broadcasted_iota(jnp.int32, (rows, rows), 0) // BLK
    key_block = lax.broadcasted_iota(jnp.int32, (rows, rows), 1) // BLK

    def split(kv):
        ones = jnp.ones((kv.shape[0], HD), jnp.bfloat16)
        return kv[:, :HD], jnp.concatenate([kv[:, HD:], ones], axis=1)

    def exponentials(queries, keys):
        scores = lax.dot_general(
            queries, keys, (((1,), (1,)), ((), ())), preferred_element_type=jnp.float32
        )
        return jnp.exp2(scores * scale)

    keys, values = split(own_ref[0])
    for stream in range(streams):
        if stream:
            self_keys, self_values = split(own_ref[stream])
        for head in range(heads):
            raw = raw_ref[stream * rows : (stream + 1) * rows, head * HD : (head + 1) * HD]
            queries = (raw * inverse_rms(raw) * gain).astype(jnp.bfloat16)
            at = pl.ds((stream * heads + head) * rows, rows)
            q_ref[at] = queries
            allowed = key_block < query_block if stream else key_block <= query_block
            weights = jnp.where(allowed, exponentials(queries, keys), 0.0).astype(jnp.bfloat16)
            total = jnp.dot(weights, values, preferred_element_type=jnp.float32)
            if stream:
                weights = jnp.where(
                    key_block == query_block, exponentials(queries, self_keys), 0.0
                ).astype(jnp.bfloat16)
                total += jnp.dot(weights, self_values, preferred_element_type=jnp.float32)
            acc_ref[at] = total

    def accumulate(start, count):
        group_keys, group_values = split(kv_ref[pl.ds(start, count)].reshape(count * rows, 2 * HD))
        for tile in range(streams * heads):
            at = pl.ds(tile * rows, rows)
            weights = exponentials(q_ref[at], group_keys).astype(jnp.bfloat16)
            acc_ref[at] += jnp.dot(weights, group_values, preferred_element_type=jnp.float32)

    pairs = GROUP // 2

    def whole(step, carry):
        lax.fori_loop((step + 1) * pairs, jnp.minimum((step + 2) * pairs, pair), relay, 0)
        start = pair - (step + 1) * pairs
        for offset in range(pairs):
            arrival(2 * (start + offset) + 1 - lane).wait_recv()
        accumulate(2 * start, GROUP)
        return carry

    def last(step, carry):
        index = lax.rem(pair, pairs) - 1 - step
        arrival(2 * index + 1 - lane).wait_recv()
        accumulate(2 * index, 2)
        return carry

    lax.fori_loop(0, jnp.minimum(pairs, pair), relay, 0)

    @pl.when(lane == 1)
    def _():
        arrival(2 * pair).wait_recv()
        accumulate(2 * pair, 1)

    lax.fori_loop(0, pair // pairs, whole, 0)
    lax.fori_loop(0, lax.rem(pair, pairs), last, 0)
    for stream in range(streams):
        for head in range(heads):
            at = pl.ds((stream * heads + head) * rows, rows)
            out_ref[stream * rows : (stream + 1) * rows, head * HD : (head + 1) * HD] = (
                acc_ref[at, :HD] / acc_ref[at, HD:]
            ).astype(jnp.bfloat16)
    each_push(lambda copy: copy.wait_send())
    lax.fori_loop(0, pair, end_relay, 0)


def attend(raw, q_gain, own, streams, rows, heads, spans):
    return pl.pallas_call(
        functools.partial(attend_kernel, rows, heads, streams, spans),
        out_shape=jax.ShapeDtypeStruct((streams * rows, heads * HD), jnp.bfloat16),
        in_specs=[pl.BlockSpec(memory_space=pltpu.VMEM)] * 3,
        out_specs=pl.BlockSpec(memory_space=pltpu.VMEM),
        scratch_shapes=[
            pltpu.VMEM((spans, rows, 2 * HD), jnp.bfloat16),
            pltpu.VMEM((streams * heads * rows, HD), jnp.bfloat16),
            pltpu.VMEM((streams * heads * rows, 2 * HD), jnp.float32),
            pltpu.SemaphoreType.DMA((spans,)),
            pltpu.SemaphoreType.DMA((spans,)),
            pltpu.SemaphoreType.DMA((spans,)),
        ],
        compiler_params=pltpu.CompilerParams(
            vmem_limit_bytes=48 * 2**20, collective_id=0, has_side_effects=True
        ),
    )(raw, q_gain, own)


def project_kernel(
    rows, att_ref, w_out_ref, live_ref, clean_ref, noised_ref,
    weight_ref, taken_ref, away_ref, here_ref, sent_ref, got_ref, give_sem, take_sem, send_sem, recv_sem, load_sem,
):
    mine = lax.axis_index("copy")
    core = lax.axis_index("tp")
    depth = att_ref.shape[1]
    loads = []
    for number, owner in enumerate((mine, 1 - mine)):
        at = pl.ds(pl.multiple_of(owner * depth, depth), depth)
        load = pltpu.make_async_copy(w_out_ref.at[at], weight_ref.at[at], load_sem.at[number])
        load.start()
        loads.append(load)
    barrier = pltpu.get_barrier_semaphore()
    pl.semaphore_signal(barrier, inc=1, device_id={"copy": 1 - mine}, device_id_type=MESH)
    pl.semaphore_signal(barrier, inc=1, device_id={"tp": 1 - core}, device_id_type=MESH)
    pl.semaphore_wait(barrier, 2)

    pieces, _, width = sent_ref.shape

    def part(start):
        return pl.ds(pl.multiple_of(start, rows), rows)

    gifts = [
        pltpu.make_async_remote_copy(
            src_ref=att_ref.at[part(start)],
            dst_ref=taken_ref.at[pl.ds(number * rows, rows)],
            send_sem=give_sem.at[number],
            recv_sem=take_sem.at[number],
            device_id={"copy": 1 - mine},
            device_id_type=MESH,
        )
        for number, start in enumerate((0, (2 - mine) * rows))
    ]
    for gift in gifts:
        gift.start()

    def weight(half, owner, piece):
        return weight_ref[
            pl.ds(pl.multiple_of(owner * depth, depth), depth),
            pl.ds(pl.multiple_of((half * pieces + piece) * width, width), width),
        ]

    def product(values, half, owner, piece):
        return jnp.dot(values, weight(half, owner, piece), preferred_element_type=jnp.float32)

    kept = jnp.concatenate([att_ref[:rows], att_ref[part((1 + mine) * rows)]], axis=0)
    loads[0].wait()
    for piece in range(pieces):
        away_ref[piece] = product(kept, 1 - core, mine, piece)
    for piece in range(pieces):
        here_ref[piece] = product(kept, core, mine, piece)
    for gift in gifts:
        gift.wait_recv()
    loads[1].wait()
    taken = taken_ref[...]
    copies = []
    for piece in range(pieces):
        sent_ref[piece] = (away_ref[piece] + product(taken, 1 - core, 1 - mine, piece)).astype(jnp.bfloat16)
        copy = pltpu.make_async_remote_copy(
            src_ref=sent_ref.at[piece],
            dst_ref=got_ref.at[piece],
            send_sem=send_sem.at[piece],
            recv_sem=recv_sem.at[piece],
            device_id={"tp": 1 - core},
            device_id_type=MESH,
        )
        copy.start()
        copies.append(copy)
    for piece in range(pieces):
        here_ref[piece] += product(taken, core, 1 - mine, piece)
    for piece, copy in enumerate(copies):
        copy.wait_recv()
        total = here_ref[piece] + got_ref[piece].astype(jnp.float32)
        at = pl.ds(piece * width, width)
        clean_ref[:, at] = total[:rows].astype(jnp.bfloat16)
        noised_ref[:, at] = (total[rows:] * live_ref[...]).astype(jnp.bfloat16)
    for copy in gifts + copies:
        copy.wait_send()


def project(attended, w_out, live_rows):
    rows = live_rows.shape[0]
    half = w_out.shape[1] // 2
    pieces = 4
    width = half // pieces
    out = jax.ShapeDtypeStruct((rows, half), jnp.bfloat16)
    return pl.pallas_call(
        functools.partial(project_kernel, rows),
        out_shape=(out, out),
        in_specs=[
            pl.BlockSpec(memory_space=pltpu.VMEM),
            pl.BlockSpec(memory_space=pltpu.HBM),
            pl.BlockSpec(memory_space=pltpu.VMEM),
        ],
        out_specs=(pl.BlockSpec(memory_space=pltpu.VMEM),) * 2,
        scratch_shapes=[
            pltpu.VMEM(w_out.shape, jnp.bfloat16),
            pltpu.VMEM((2 * rows, attended.shape[1]), jnp.bfloat16),
            pltpu.VMEM((pieces, 2 * rows, width), jnp.float32),
            pltpu.VMEM((pieces, 2 * rows, width), jnp.float32),
            pltpu.VMEM((pieces, 2 * rows, width), jnp.bfloat16),
            pltpu.VMEM((pieces, 2 * rows, width), jnp.bfloat16),
            pltpu.SemaphoreType.DMA((2,)),
            pltpu.SemaphoreType.DMA((2,)),
            pltpu.SemaphoreType.DMA((pieces,)),
            pltpu.SemaphoreType.DMA((pieces,)),
            pltpu.SemaphoreType.DMA((2,)),
        ],
        compiler_params=pltpu.CompilerParams(
            vmem_limit_bytes=44 * 2**20, collective_id=1, has_side_effects=True
        ),
    )(attended, w_out, live_rows)


SWAP = [(0, 1), (1, 0)]


def on_device(
    clean_tokens,
    norm_gain,
    mask_embed,
    time_shift,
    w_query,
    w_key,
    w_value,
    w_out,
    q_gain,
    k_gain,
    masked,
    block_live,
    timesteps,
):
    mine = lax.axis_index("copy")
    core = lax.axis_index("tp")
    first = mine == 0
    rows = clean_tokens.shape[0]
    streams = 3
    q_width = w_query.shape[1] // 2
    heads = q_width // HD

    def ordered(own, other, axis):
        return jnp.where(
            first,
            jnp.concatenate([own, other], axis=axis),
            jnp.concatenate([other, own], axis=axis),
        )

    notes = jnp.concatenate([masked, timesteps[:, None]], axis=1)
    other_notes = lax.ppermute(notes, "copy", SWAP)
    near_rows = lax.ppermute(
        lax.dynamic_slice_in_dim(clean_tokens, core * (rows // 2), rows // 2, axis=0), "copy", SWAP
    )
    far_rows = lax.ppermute(near_rows, "tp", SWAP)
    other_tokens = jnp.where(
        core == 0,
        jnp.concatenate([near_rows, far_rows], axis=0),
        jnp.concatenate([far_rows, near_rows], axis=0),
    )
    query_weight = lax.dynamic_slice_in_dim(w_query, mine * q_width, q_width, axis=1)
    pair_weight = jnp.concatenate(
        [
            lax.dynamic_slice_in_dim(w_key, mine * HD, HD, axis=1),
            lax.dynamic_slice_in_dim(w_value, mine * HD, HD, axis=1),
        ],
        axis=1,
    )
    features = ordered(clean_tokens, other_tokens, 1).astype(jnp.float32)
    both_notes = ordered(notes, other_notes, 0)
    gain = norm_gain.astype(jnp.float32)
    base = features * inverse_rms(features) * gain
    mask_wide = mask_embed.astype(jnp.float32)[None, :]
    mask_base = mask_wide * inverse_rms(mask_wide) * gain
    condition = (
        1.0 + both_notes[:, rows:].astype(jnp.float32)[:, :, None] / TSTEPS * time_shift[None, None, :]
    )
    condition = jnp.concatenate([jnp.ones_like(condition[:1]), condition], axis=0)
    hidden = jnp.concatenate([jnp.zeros_like(masked), both_notes[:, :rows]], axis=0)
    all_rows = jnp.where(hidden[:, :, None] == 1, mask_base[None], base[None]) * condition
    all_rows = all_rows.astype(jnp.bfloat16).reshape(streams * rows, -1)
    raw = jnp.dot(all_rows, query_weight, preferred_element_type=jnp.float32)
    wide = jnp.dot(all_rows, pair_weight, preferred_element_type=jnp.float32)
    key_wide = wide[:, :HD]
    keys = (key_wide * inverse_rms(key_wide) * k_gain).astype(jnp.bfloat16)
    values = wide[:, HD:].astype(jnp.bfloat16)
    own = jnp.concatenate([keys, values], axis=1).reshape(streams, rows, 2 * HD)
    spans = lax.axis_size("ctx")
    attended = attend(raw, q_gain[None, :], own, streams, rows, heads, spans)
    live_rows = jnp.repeat(block_live[0], BLK)[:, None].astype(jnp.float32)
    clean_out, noised_out = project(attended, w_out, live_rows)
    noised_out = noised_out[None]
    return (clean_out, noised_out)


def solution(mesh):
    in_specs = (
        P("ctx", "copy"),
        P(),
        P(),
        P(),
        P(None, "tp"),
        P(None, "tp"),
        P(None, "tp"),
        P("tp", None),
        P(),
        P(),
        P("copy", "ctx"),
        P("copy", "ctx"),
        P("copy"),
    )
    out_specs = (P("ctx", "tp"), P("copy", "ctx", "tp"))
    return jax.shard_map(
        on_device, mesh=mesh, in_specs=in_specs, out_specs=out_specs, check_vma=False
    )
```

```python
import functools
import math

import jax
import jax.numpy as jnp
from jax import lax
from jax.experimental import pallas as pl
from jax.experimental.pallas import tpu as pltpu
from jax.sharding import PartitionSpec as P

HD = 128
BLK = 64
TSTEPS = 1000
EPS = 1e-06
GROUP = 4
SIDE = 4
MESH = pl.DeviceIdType.MESH


def inverse_rms(values):
    return lax.rsqrt(jnp.mean(values * values, axis=-1, keepdims=True) + EPS)


def attend_kernel(
    rows, heads, streams, spans, row_ref, w_query_ref, gain_ref, own_ref, out_ref,
    weight_ref, kv_ref, q_ref, acc_ref, send_sem, recv_sem, forward_sem, load_sem,
):
    me = lax.axis_index("ctx")

    barrier = pltpu.get_barrier_semaphore()

    def greet(step, carry):
        pl.semaphore_signal(
            barrier, inc=1, device_id={"ctx": lax.rem(me + step, spans)}, device_id_type=MESH
        )
        return carry

    lax.fori_loop(1, spans, greet, 0)
    pl.semaphore_wait(barrier, spans - 1)

    def push(target):
        return pltpu.make_async_remote_copy(
            src_ref=own_ref.at[0],
            dst_ref=kv_ref.at[me],
            send_sem=send_sem.at[target],
            recv_sem=recv_sem.at[me],
            device_id={"ctx": target},
            device_id_type=MESH,
        )

    def arrival(source):
        return pltpu.make_async_remote_copy(
            src_ref=own_ref.at[0],
            dst_ref=kv_ref.at[source],
            send_sem=send_sem.at[source],
            recv_sem=recv_sem.at[source],
            device_id={"ctx": source},
            device_id_type=MESH,
        )

    pair = me // 2
    lane = lax.rem(me, 2)
    partner = me + 1 - 2 * lane

    def relayed(index):
        return lax.rem(index, 4) != 3

    def each_push(act):
        @pl.when(lane == 0)
        def _():
            act(push(partner))

        def to_pair(step, carry):
            index = SIDE * (SIDE - 1 - step // SIDE) + lax.rem(pair + 1 + lax.rem(step, SIDE), SIDE)

            @pl.when(index > pair)
            def _():
                act(push(2 * index + lane))

            @pl.when(jnp.logical_and(index > pair, jnp.logical_not(relayed(pair))))
            def _():
                act(push(2 * index + 1 - lane))

            return carry

        lax.fori_loop(0, SIDE * SIDE, to_pair, 0)

    def forward(index):
        slot = 2 * index + lane
        return pltpu.make_async_remote_copy(
            src_ref=kv_ref.at[slot],
            dst_ref=kv_ref.at[slot],
            send_sem=forward_sem.at[slot],
            recv_sem=recv_sem.at[slot],
            device_id={"ctx": partner},
            device_id_type=MESH,
        )

    def relay(step, carry):
        index = pair - 1 - step
        arrival(2 * index + lane).wait_recv()

        @pl.when(relayed(index))
        def _():
            forward(index).start()

        return carry

    def end_relay(index, carry):
        @pl.when(relayed(index))
        def _():
            forward(index).wait_send()

        return carry

    load = pltpu.make_async_copy(w_query_ref, weight_ref, load_sem)
    load.start()
    each_push(lambda copy: copy.start())
    scale = math.log2(math.e) / math.sqrt(HD)
    gain = gain_ref[...]
    query_block = lax.broadcasted_iota(jnp.int32, (rows, rows), 0) // BLK
    key_block = lax.broadcasted_iota(jnp.int32, (rows, rows), 1) // BLK

    def split(kv):
        ones = jnp.ones((kv.shape[0], HD), jnp.bfloat16)
        return kv[:, :HD], jnp.concatenate([kv[:, HD:], ones], axis=1)

    def exponentials(queries, keys):
        scores = lax.dot_general(
            queries, keys, (((1,), (1,)), ((), ())), preferred_element_type=jnp.float32
        )
        return jnp.exp2(scores * scale)

    load.wait()
    keys, values = split(own_ref[0])
    for stream in range(streams):
        if stream:
            self_keys, self_values = split(own_ref[stream])
        wide = jnp.dot(
            row_ref[stream * rows : (stream + 1) * rows],
            weight_ref[...],
            preferred_element_type=jnp.float32,
        )
        for head in range(heads):
            raw = wide[:, head * HD : (head + 1) * HD]
            queries = (raw * inverse_rms(raw) * gain).astype(jnp.bfloat16)
            at = pl.ds((stream * heads + head) * rows, rows)
            q_ref[at] = queries
            allowed = key_block < query_block if stream else key_block <= query_block
            weights = jnp.where(allowed, exponentials(queries, keys), 0.0).astype(jnp.bfloat16)
            total = jnp.dot(weights, values, preferred_element_type=jnp.float32)
            if stream:
                weights = jnp.where(
                    key_block == query_block, exponentials(queries, self_keys), 0.0
                ).astype(jnp.bfloat16)
                total += jnp.dot(weights, self_values, preferred_element_type=jnp.float32)
            acc_ref[at] = total

    def accumulate(start, count):
        group_keys, group_values = split(kv_ref[pl.ds(start, count)].reshape(count * rows, 2 * HD))
        for tile in range(streams * heads):
            at = pl.ds(tile * rows, rows)
            weights = exponentials(q_ref[at], group_keys).astype(jnp.bfloat16)
            acc_ref[at] += jnp.dot(weights, group_values, preferred_element_type=jnp.float32)

    pairs = GROUP // 2

    def whole(step, carry):
        lax.fori_loop((step + 1) * pairs, jnp.minimum((step + 2) * pairs, pair), relay, 0)
        start = pair - (step + 1) * pairs
        for offset in range(pairs):
            arrival(2 * (start + offset) + 1 - lane).wait_recv()
        accumulate(2 * start, GROUP)
        return carry

    def last(step, carry):
        index = lax.rem(pair, pairs) - 1 - step
        arrival(2 * index + 1 - lane).wait_recv()
        accumulate(2 * index, 2)
        return carry

    lax.fori_loop(0, jnp.minimum(pairs, pair), relay, 0)

    @pl.when(lane == 1)
    def _():
        arrival(2 * pair).wait_recv()
        accumulate(2 * pair, 1)

    lax.fori_loop(0, pair // pairs, whole, 0)
    lax.fori_loop(0, lax.rem(pair, pairs), last, 0)
    for stream in range(streams):
        for head in range(heads):
            at = pl.ds((stream * heads + head) * rows, rows)
            out_ref[stream * rows : (stream + 1) * rows, head * HD : (head + 1) * HD] = (
                acc_ref[at, :HD] / acc_ref[at, HD:]
            ).astype(jnp.bfloat16)
    each_push(lambda copy: copy.wait_send())
    lax.fori_loop(0, pair, end_relay, 0)


def attend(all_rows, query_weight, q_gain, own, streams, rows, heads, spans):
    return pl.pallas_call(
        functools.partial(attend_kernel, rows, heads, streams, spans),
        out_shape=jax.ShapeDtypeStruct((streams * rows, heads * HD), jnp.bfloat16),
        in_specs=[
            pl.BlockSpec(memory_space=pltpu.VMEM),
            pl.BlockSpec(memory_space=pltpu.HBM),
            pl.BlockSpec(memory_space=pltpu.VMEM),
            pl.BlockSpec(memory_space=pltpu.VMEM),
        ],
        out_specs=pl.BlockSpec(memory_space=pltpu.VMEM),
        scratch_shapes=[
            pltpu.VMEM(query_weight.shape, jnp.bfloat16),
            pltpu.VMEM((spans, rows, 2 * HD), jnp.bfloat16),
            pltpu.VMEM((streams * heads * rows, HD), jnp.bfloat16),
            pltpu.VMEM((streams * heads * rows, 2 * HD), jnp.float32),
            pltpu.SemaphoreType.DMA((spans,)),
            pltpu.SemaphoreType.DMA((spans,)),
            pltpu.SemaphoreType.DMA((spans,)),
            pltpu.SemaphoreType.DMA,
        ],
        compiler_params=pltpu.CompilerParams(
            vmem_limit_bytes=48 * 2**20, collective_id=0, has_side_effects=True
        ),
    )(all_rows, query_weight, q_gain, own)


def project_kernel(
    rows, att_ref, w_out_ref, live_ref, clean_ref, noised_ref,
    weight_ref, taken_ref, away_ref, here_ref, sent_ref, got_ref, give_sem, take_sem, send_sem, recv_sem, load_sem,
):
    mine = lax.axis_index("copy")
    core = lax.axis_index("tp")
    depth = att_ref.shape[1]
    loads = []
    for number, owner in enumerate((mine, 1 - mine)):
        at = pl.ds(pl.multiple_of(owner * depth, depth), depth)
        load = pltpu.make_async_copy(w_out_ref.at[at], weight_ref.at[at], load_sem.at[number])
        load.start()
        loads.append(load)
    barrier = pltpu.get_barrier_semaphore()
    pl.semaphore_signal(barrier, inc=1, device_id={"copy": 1 - mine}, device_id_type=MESH)
    pl.semaphore_signal(barrier, inc=1, device_id={"tp": 1 - core}, device_id_type=MESH)
    pl.semaphore_wait(barrier, 2)

    pieces, _, width = sent_ref.shape

    def part(start):
        return pl.ds(pl.multiple_of(start, rows), rows)

    gifts = [
        pltpu.make_async_remote_copy(
            src_ref=att_ref.at[part(start)],
            dst_ref=taken_ref.at[pl.ds(number * rows, rows)],
            send_sem=give_sem.at[number],
            recv_sem=take_sem.at[number],
            device_id={"copy": 1 - mine},
            device_id_type=MESH,
        )
        for number, start in enumerate((0, (2 - mine) * rows))
    ]
    for gift in gifts:
        gift.start()

    def weight(half, owner, piece):
        return weight_ref[
            pl.ds(pl.multiple_of(owner * depth, depth), depth),
            pl.ds(pl.multiple_of((half * pieces + piece) * width, width), width),
        ]

    def product(values, half, owner, piece):
        return jnp.dot(values, weight(half, owner, piece), preferred_element_type=jnp.float32)

    kept = jnp.concatenate([att_ref[:rows], att_ref[part((1 + mine) * rows)]], axis=0)
    loads[0].wait()
    for piece in range(pieces):
        away_ref[piece] = product(kept, 1 - core, mine, piece)
    for piece in range(pieces):
        here_ref[piece] = product(kept, core, mine, piece)
    for gift in gifts:
        gift.wait_recv()
    loads[1].wait()
    taken = taken_ref[...]
    copies = []
    for piece in range(pieces):
        sent_ref[piece] = (away_ref[piece] + product(taken, 1 - core, 1 - mine, piece)).astype(jnp.bfloat16)
        copy = pltpu.make_async_remote_copy(
            src_ref=sent_ref.at[piece],
            dst_ref=got_ref.at[piece],
            send_sem=send_sem.at[piece],
            recv_sem=recv_sem.at[piece],
            device_id={"tp": 1 - core},
            device_id_type=MESH,
        )
        copy.start()
        copies.append(copy)
    for piece in range(pieces):
        here_ref[piece] += product(taken, core, 1 - mine, piece)
    for piece, copy in enumerate(copies):
        copy.wait_recv()
        total = here_ref[piece] + got_ref[piece].astype(jnp.float32)
        at = pl.ds(piece * width, width)
        clean_ref[:, at] = total[:rows].astype(jnp.bfloat16)
        noised_ref[:, at] = (total[rows:] * live_ref[...]).astype(jnp.bfloat16)
    for copy in gifts + copies:
        copy.wait_send()


def project(attended, w_out, live_rows):
    rows = live_rows.shape[0]
    half = w_out.shape[1] // 2
    pieces = 4
    width = half // pieces
    out = jax.ShapeDtypeStruct((rows, half), jnp.bfloat16)
    return pl.pallas_call(
        functools.partial(project_kernel, rows),
        out_shape=(out, out),
        in_specs=[
            pl.BlockSpec(memory_space=pltpu.VMEM),
            pl.BlockSpec(memory_space=pltpu.HBM),
            pl.BlockSpec(memory_space=pltpu.VMEM),
        ],
        out_specs=(pl.BlockSpec(memory_space=pltpu.VMEM),) * 2,
        scratch_shapes=[
            pltpu.VMEM(w_out.shape, jnp.bfloat16),
            pltpu.VMEM((2 * rows, attended.shape[1]), jnp.bfloat16),
            pltpu.VMEM((pieces, 2 * rows, width), jnp.float32),
            pltpu.VMEM((pieces, 2 * rows, width), jnp.float32),
            pltpu.VMEM((pieces, 2 * rows, width), jnp.bfloat16),
            pltpu.VMEM((pieces, 2 * rows, width), jnp.bfloat16),
            pltpu.SemaphoreType.DMA((2,)),
            pltpu.SemaphoreType.DMA((2,)),
            pltpu.SemaphoreType.DMA((pieces,)),
            pltpu.SemaphoreType.DMA((pieces,)),
            pltpu.SemaphoreType.DMA((2,)),
        ],
        compiler_params=pltpu.CompilerParams(
            vmem_limit_bytes=44 * 2**20, collective_id=1, has_side_effects=True
        ),
    )(attended, w_out, live_rows)


SWAP = [(0, 1), (1, 0)]


def on_device(
    clean_tokens,
    norm_gain,
    mask_embed,
    time_shift,
    w_query,
    w_key,
    w_value,
    w_out,
    q_gain,
    k_gain,
    masked,
    block_live,
    timesteps,
):
    mine = lax.axis_index("copy")
    core = lax.axis_index("tp")
    first = mine == 0
    rows = clean_tokens.shape[0]
    streams = 3
    q_width = w_query.shape[1] // 2
    heads = q_width // HD

    def ordered(own, other, axis):
        return jnp.where(
            first,
            jnp.concatenate([own, other], axis=axis),
            jnp.concatenate([other, own], axis=axis),
        )

    notes = jnp.concatenate([masked, timesteps[:, None]], axis=1)
    other_notes = lax.ppermute(notes, "copy", SWAP)
    near_rows = lax.ppermute(
        lax.dynamic_slice_in_dim(clean_tokens, core * (rows // 2), rows // 2, axis=0), "copy", SWAP
    )
    far_rows = lax.ppermute(near_rows, "tp", SWAP)
    other_tokens = jnp.where(
        core == 0,
        jnp.concatenate([near_rows, far_rows], axis=0),
        jnp.concatenate([far_rows, near_rows], axis=0),
    )
    query_weight = lax.dynamic_slice_in_dim(w_query, mine * q_width, q_width, axis=1)
    pair_weight = jnp.concatenate(
        [
            lax.dynamic_slice_in_dim(w_key, mine * HD, HD, axis=1),
            lax.dynamic_slice_in_dim(w_value, mine * HD, HD, axis=1),
        ],
        axis=1,
    )
    features = ordered(clean_tokens, other_tokens, 1).astype(jnp.float32)
    both_notes = ordered(notes, other_notes, 0)
    gain = norm_gain.astype(jnp.float32)
    base = features * inverse_rms(features) * gain
    mask_wide = mask_embed.astype(jnp.float32)[None, :]
    mask_base = mask_wide * inverse_rms(mask_wide) * gain
    condition = (
        1.0 + both_notes[:, rows:].astype(jnp.float32)[:, :, None] / TSTEPS * time_shift[None, None, :]
    )
    condition = jnp.concatenate([jnp.ones_like(condition[:1]), condition], axis=0)
    hidden = jnp.concatenate([jnp.zeros_like(masked), both_notes[:, :rows]], axis=0)
    all_rows = jnp.where(hidden[:, :, None] == 1, mask_base[None], base[None]) * condition
    all_rows = all_rows.astype(jnp.bfloat16).reshape(streams * rows, -1)
    wide = jnp.dot(all_rows, pair_weight, preferred_element_type=jnp.float32)
    key_wide = wide[:, :HD]
    keys = (key_wide * inverse_rms(key_wide) * k_gain).astype(jnp.bfloat16)
    values = wide[:, HD:].astype(jnp.bfloat16)
    own = jnp.concatenate([keys, values], axis=1).reshape(streams, rows, 2 * HD)
    spans = lax.axis_size("ctx")
    attended = attend(all_rows, query_weight, q_gain[None, :], own, streams, rows, heads, spans)
    live_rows = jnp.repeat(block_live[0], BLK)[:, None].astype(jnp.float32)
    clean_out, noised_out = project(attended, w_out, live_rows)
    noised_out = noised_out[None]
    return (clean_out, noised_out)


def solution(mesh):
    in_specs = (
        P("ctx", "copy"),
        P(),
        P(),
        P(),
        P(None, "tp"),
        P(None, "tp"),
        P(None, "tp"),
        P("tp", None),
        P(),
        P(),
        P("copy", "ctx"),
        P("copy", "ctx"),
        P("copy"),
    )
    out_specs = (P("ctx", "tp"), P("copy", "ctx", "tp"))
    return jax.shard_map(
        on_device, mesh=mesh, in_specs=in_specs, out_specs=out_specs, check_vma=False
    )
```
